32 devices in a mesh: fsdp: 8 (over y, x, core), tp: 4 (over z).
Axes of the slice: x: 2, y: 2, z: 4, core: 2. Of those that a mesh axis runs over, the one named last changes fastest.
Arguments:
- tokens: bfloat16 [3, 16, 1024, 1024], P(None, 'fsdp', 'tp'), may hold values from -6 to 6
- encoded: bfloat16 [16, 512, 1024], P('fsdp', 'tp'), may hold values from -6 to 6
- out_cotangent: bfloat16 [3, 16, 1024, 1024], P(None, 'fsdp', 'tp'), may hold values from -6 to 6
- segment_start: int32 [16, 13], P('fsdp'), may hold values from 0 to 1023, as said below
- segment_parent: int32 [16, 13], P('fsdp'), may hold values from 0 to 4, as said below
- query_weight: bfloat16 [1024, 1024], P('fsdp', 'tp'), may hold values from -0.1875 to 0.1875
- key_weight: bfloat16 [1024, 1024], P('fsdp', 'tp'), may hold values from -0.1875 to 0.1875
- value_weight: bfloat16 [1024, 1024], P('fsdp', 'tp'), may hold values from -0.1875 to 0.1875
- out_weight: bfloat16 [1024, 1024], P('tp', 'fsdp'), may hold values from -0.75 to 0.75
- cross_query: bfloat16 [1024, 1024], P('fsdp', 'tp'), may hold values from -0.1875 to 0.1875
- cross_key: bfloat16 [1024, 1024], P('fsdp', 'tp'), may hold values from -0.1875 to 0.1875
- cross_value: bfloat16 [1024, 1024], P('fsdp', 'tp'), may hold values from -0.1875 to 0.1875
- cross_out: bfloat16 [1024, 1024], P('tp', 'fsdp'), may hold values from -0.75 to 0.75
- expand_weight: bfloat16 [1024, 4096], P('fsdp', 'tp'), may hold values from -0.1875 to 0.1875
- expand_bias: float32 [4096], P('tp'), may hold values from -3 to 3
- reduce_weight: bfloat16 [4096, 1024], P('tp', 'fsdp'), may hold values from -0.09375 to 0.09375
- reduce_bias: float32 [1024], replicated, may hold values from -2 to 2
- norm_gain: float32 [3, 1024], replicated, may hold values from 0.5 to 1.5
- norm_bias: float32 [3, 1024], replicated, may hold values from -2 to 2
- bucket_table: float32 [32, 16], P(None, 'tp'), may hold values from -3 to 3
Outputs:
- layer_out: float32 [3, 16, 1024, 1024], P(None, 'fsdp', 'tp')
- tokens_grad: float32 [3, 16, 1024, 1024], P(None, 'fsdp', 'tp')
- encoded_grad: float32 [16, 512, 1024], P('fsdp', 'tp')
- grad_query_weight: float32 [1024, 1024], P('fsdp', 'tp')
- grad_key_weight: float32 [1024, 1024], P('fsdp', 'tp')
- grad_value_weight: float32 [1024, 1024], P('fsdp', 'tp')
- grad_out_weight: float32 [1024, 1024], P('tp', 'fsdp')
- grad_cross_query: float32 [1024, 1024], P('fsdp', 'tp')
- grad_cross_key: float32 [1024, 1024], P('fsdp', 'tp')
- grad_cross_value: float32 [1024, 1024], P('fsdp', 'tp')
- grad_cross_out: float32 [1024, 1024], P('tp', 'fsdp')
- grad_expand_weight: float32 [1024, 4096], P('fsdp', 'tp')
- grad_expand_bias: float32 [4096], P('tp')
- grad_reduce_weight: float32 [4096, 1024], P('tp', 'fsdp')
- grad_reduce_bias: float32 [1024], replicated
- grad_norm_gain: float32 [3, 1024], replicated
- grad_norm_bias: float32 [3, 1024], replicated
- grad_bucket_table: float32 [32, 16], P(None, 'tp')
The draws below stay inside these ranges and needn't reach their ends.
Inputs may be any that keep to these rules, and one draw needn't show every extreme that they name: `segment_start`: in each tree the starts do not fall; the first is 0 and the second is 256. `segment_parent`: segment 0 is the trunk and names itself; segments 1 to 4 name 0; every later segment names one of 1 to 4.
All inputs are finite; a program needn't handle non-finite values.
Results may differ from the reference program's by a relative error of at most 0.033.
Values may be sent and summed in bfloat16 or wider, within the bound.
A program may use at most 640 MiB of HBM per device.

```python
import jax
import jax.numpy as jnp
from jax import lax

D = 1024
HEADS = 16
HEAD_DIM = 64
FF = 4096
NB = 32
STREAMS = 3
BRANCHES = 4
SEGS = 13
TREE = 1024
TRUNK = 256
ENC = 512
TREES = 16
N_TP = 4


def draw_segment_start(key, part):
    cut_points = jax.random.randint(jax.random.fold_in(key, 11), (TREES, SEGS - 2), 0, TREE - TRUNK)
    cut_points = jnp.sort(cut_points, axis=1)
    leading = jnp.zeros((TREES, 1), jnp.int32)
    trunk_end = jnp.full((TREES, 1), TRUNK, jnp.int32)
    return jnp.concatenate([leading, trunk_end, TRUNK + cut_points], axis=1).astype(jnp.int32)


def draw_segment_parent(key, part):
    parent_pick = jax.random.randint(jax.random.fold_in(key, 12), (TREES, SEGS - 1 - BRANCHES), 1, BRANCHES + 1)
    leading = jnp.zeros((TREES, 1 + BRANCHES), jnp.int32)
    return jnp.concatenate([leading, parent_pick], axis=1).astype(jnp.int32)


def block_scale(stream_key, dims, cuts, smallest, high):
    def one(dim, blocks):
        heights = jax.random.uniform(jax.random.fold_in(jax.random.fold_in(stream_key, 6), dim), (blocks,), jnp.float32, smallest / len(cuts), high / len(cuts))
        return jnp.repeat(jnp.exp(heights), dims[dim] // blocks).reshape((-1,) + (1,) * (len(dims) - dim - 1))

    loudness = one(*cuts[0])
    for cut in cuts[1:]:
        loudness = loudness * one(*cut)
    return loudness


def gaussian(stream_key, extent, scale, reach, split=(), kind=jnp.bfloat16):
    array = scale * jax.random.normal(stream_key, extent, jnp.float32)
    if split:
        array = array * block_scale(stream_key, extent, split, -0.22, 0.18)
    return jnp.clip(array, -reach, reach).astype(kind)


def setup_inputs(seed: int = 0) -> dict:
    streams_of = jax.random.split(jax.random.key(seed), 21)
    tokens = gaussian(streams_of[0], (STREAMS, TREES, TREE, D), 1.0, 6.0, ((1, 8), (2, 4)))
    encoded = gaussian(streams_of[1], (TREES, ENC, D), 1.0, 6.0, ((0, 8), (1, 4)))
    out_cotangent = gaussian(streams_of[2], (STREAMS, TREES, TREE, D), 1.0, 6.0, ((1, 8), (2, 4)))
    segment_start = draw_segment_start(jax.random.fold_in(streams_of[20], 71), 0)
    segment_parent = draw_segment_parent(jax.random.fold_in(streams_of[20], 71), 0)
    query_weight = gaussian(streams_of[5], (D, D), D ** -0.5, 0.1875, ((0, 8), (1, 4)))
    key_weight = gaussian(streams_of[6], (D, D), D ** -0.5, 0.1875, ((0, 8), (1, 4)))
    value_weight = gaussian(streams_of[7], (D, D), D ** -0.5, 0.1875, ((0, 8), (1, 4)))
    out_weight = gaussian(streams_of[8], (D, D), (D // 16) ** -0.5, 0.75, ((0, 4), (1, 8)))
    cross_query = gaussian(streams_of[9], (D, D), D ** -0.5, 0.1875, ((0, 8), (1, 4)))
    cross_key = gaussian(streams_of[10], (D, D), D ** -0.5, 0.1875, ((0, 8), (1, 4)))
    cross_value = gaussian(streams_of[11], (D, D), D ** -0.5, 0.1875, ((0, 8), (1, 4)))
    cross_out = gaussian(streams_of[12], (D, D), (D // 16) ** -0.5, 0.75, ((0, 4), (1, 8)))
    expand_weight = gaussian(streams_of[13], (D, FF), D ** -0.5, 0.1875, ((0, 8), (1, 4)))
    expand_bias = gaussian(streams_of[14], (FF,), 0.5, 3.0, ((0, 4),), jnp.float32)
    reduce_weight = gaussian(streams_of[15], (FF, D), FF ** -0.5, 0.09375, ((0, 4), (1, 8)))
    reduce_bias = gaussian(streams_of[16], (D,), 0.3, 2.0, (), jnp.float32)
    norm_gain = jnp.clip(1.0 + 0.1 * jax.random.normal(streams_of[17], (3, D), jnp.float32), 0.5, 1.5)
    norm_bias = gaussian(streams_of[18], (3, D), 0.3, 2.0, (), jnp.float32)
    bucket_table = gaussian(streams_of[19], (NB, HEADS), 0.7, 3.0, ((1, 4),), jnp.float32)
    return dict(tokens=tokens, encoded=encoded, out_cotangent=out_cotangent, segment_start=segment_start, segment_parent=segment_parent, query_weight=query_weight, key_weight=key_weight, value_weight=value_weight, out_weight=out_weight, cross_query=cross_query, cross_key=cross_key, cross_value=cross_value, cross_out=cross_out, expand_weight=expand_weight, expand_bias=expand_bias, reduce_weight=reduce_weight, reduce_bias=reduce_bias, norm_gain=norm_gain, norm_bias=norm_bias, bucket_table=bucket_table)


@jax.custom_vjp
def low(v):
    return lax.optimization_barrier(v.astype(jnp.bfloat16)).astype(jnp.float32)

@jax.custom_vjp
def low_back(v):
    return v

def low_keep(v):
    return (low(v), None)

def low_pass(kept, grad):
    return (grad,)

def back_keep(v):
    return (v, None)

def back_low(kept, grad):
    return (low(grad),)
low.defvjp(low_keep, low_pass)
low_back.defvjp(back_keep, back_low)
highest = lax.Precision.HIGHEST
edge_list = (16, 18, 21, 24, 27, 31, 35, 40, 45, 52, 59, 67, 76, 87, 99, 112)
norm_eps = 1e-05
masked_value = -1000000000.0

def both_ways(value):
    return low(low_back(value))

def tree_layout(offsets, parents):
    position = jnp.arange(TREE, dtype=jnp.int32)
    segment_count = offsets.shape[0]
    segment = lax.optimization_barrier(jnp.sum((position[:, None] >= offsets[None, 1:]).astype(jnp.int32), axis=1))
    segment_ids = jnp.arange(segment_count, dtype=jnp.int32)
    ending = jnp.concatenate([offsets[1:], jnp.full((1,), TREE, jnp.int32)])
    segment_length = (ending - offsets).astype(jnp.float32)
    identity = (segment_ids[:, None] == segment_ids[None, :]).astype(jnp.float32)
    upward = (parents[:, None] == segment_ids[None, :]).astype(jnp.float32)
    grand = lax.optimization_barrier(jnp.sum(upward[:, :, None] * upward[None, :, :], axis=1))
    ancestry = jnp.minimum(identity + upward + grand, 1.0)
    depth_start = lax.optimization_barrier(jnp.sum((ancestry - identity) * segment_length[None, :], axis=1))
    token_start = (position - offsets[segment]).astype(jnp.float32)
    path_depth = token_start + depth_start[segment]
    reach_rows = ancestry[segment]
    reach_value = reach_rows[:, segment]
    distance = jnp.maximum(path_depth[:, None] - path_depth[None, :], 0.0)
    return (reach_value > 0.5, distance)

def bucket_of(distance):
    crossed = jnp.zeros_like(distance)
    for edge_value in edge_list:
        crossed = crossed + (distance >= edge_value).astype(distance.dtype)
    return jnp.where(distance < 16.0, distance, 15.0 + crossed)

def layer_norm(summed, gain_row, shift_row):
    center = summed - lax.optimization_barrier(jnp.mean(summed, axis=-1, keepdims=True))
    spread = lax.optimization_barrier(jnp.mean(center * center, axis=-1, keepdims=True))
    return center * lax.rsqrt(spread + norm_eps) * gain_row + shift_row

def project(row_block, weight):
    return jnp.einsum('std,de->ste', row_block, weight, precision=highest)

def output_sum(mixed_heads, weight):
    share_rows = weight.shape[0] // N_TP
    running = jnp.zeros(mixed_heads.shape[:2] + (weight.shape[1],), jnp.float32)
    for tp_index in range(N_TP):
        lower_row = tp_index * share_rows
        running = running + low(project(mixed_heads[:, :, lower_row:lower_row + share_rows], weight[lower_row:lower_row + share_rows]))
    return low_back(running)

def self_attention(inputs, query_weight, key_weight, value_weight, out_weight, bucket_table, reachable, distance):
    rounded = low(inputs)
    query_heads = both_ways(project(rounded, low(query_weight))).reshape(STREAMS, TREE, HEADS, HEAD_DIM)
    key_heads = both_ways(project(rounded, low(key_weight))).reshape(STREAMS, TREE, HEADS, HEAD_DIM)
    value_heads = both_ways(project(rounded, low(value_weight))).reshape(STREAMS, TREE, HEADS, HEAD_DIM)
    onehot = (bucket_of(distance)[:, :, None] == jnp.arange(NB, dtype=jnp.float32)[None, None, :]).astype(jnp.float32)
    bias_full = jnp.einsum('qkb,bh->hqk', onehot, bucket_table, precision=highest)
    score_scale = HEAD_DIM ** (-0.5)
    position = jnp.arange(TREE, dtype=jnp.int32)
    causal = reachable & (position[None, :] <= position[:, None])
    strict = reachable & (position[None, :] < position[:, None])
    attended_list = []
    for stream in range(STREAMS):
        raw_scores = low_back(jnp.einsum('qhe,khe->hqk', query_heads[stream], key_heads[0], precision=highest) * score_scale)
        allowed = causal if stream == 0 else strict
        logits = jnp.where(allowed[None], raw_scores + bias_full, masked_value)
        own_raw = lax.optimization_barrier(jnp.sum(query_heads[stream] * key_heads[stream], axis=-1)).T * score_scale + bucket_table[0][:, None]
        own_logit = own_raw if stream > 0 else jnp.full_like(own_raw, masked_value)
        top_value = jnp.maximum(lax.optimization_barrier(jnp.max(logits, axis=-1)), own_logit)
        main_part = jnp.exp(logits - top_value[..., None])
        own_part = jnp.exp(own_logit - top_value)
        denominator = lax.optimization_barrier(jnp.sum(main_part, axis=-1)) + own_part
        attended = jnp.einsum('hqk,khe->qhe', low(main_part / denominator[..., None]), value_heads[0], precision=highest)
        attended = attended + (own_part / denominator).T[:, :, None] * value_heads[stream]
        attended_list.append(attended.reshape(TREE, HEADS * HEAD_DIM))
    mixed_heads = both_ways(jnp.stack(attended_list))
    return output_sum(mixed_heads, low(out_weight))

def cross_attention(inputs, encoded, cross_query, cross_key, cross_value, cross_out):
    query_heads = both_ways(project(low(inputs), low(cross_query))).reshape(STREAMS, TREE, HEADS, HEAD_DIM)
    encoder_low = low(encoded)
    key_heads = both_ways(jnp.dot(encoder_low, low(cross_key), precision=highest)).reshape(ENC, HEADS, HEAD_DIM)
    value_heads = both_ways(jnp.dot(encoder_low, low(cross_value), precision=highest)).reshape(ENC, HEADS, HEAD_DIM)
    score_scale = HEAD_DIM ** (-0.5)
    raw_scores = low_back(jnp.einsum('sqhe,khe->shqk', query_heads, key_heads, precision=highest) * score_scale)
    top_value = lax.optimization_barrier(jnp.max(raw_scores, axis=-1, keepdims=True))
    main_part = jnp.exp(raw_scores - top_value)
    prob_main = main_part / lax.optimization_barrier(jnp.sum(main_part, axis=-1, keepdims=True))
    attended = jnp.einsum('shqk,khe->sqhe', low(prob_main), value_heads, precision=highest)
    mixed_heads = both_ways(attended.reshape(STREAMS, TREE, D))
    return output_sum(mixed_heads, low(cross_out))

def feed_forward(inputs, expand_weight, expand_bias, reduce_weight):
    before = low_back(project(low(inputs), low(expand_weight))) + expand_bias
    hidden = low(jax.nn.gelu(before, approximate=False))
    return output_sum(hidden, low(reduce_weight))

def tree_forward(inputs, encoded, params, reachable, distance):
    query_weight, key_weight, value_weight, out_weight, cross_query, cross_key, cross_value, cross_out, expand_weight, expand_bias, reduce_weight, reduce_bias, norm_gain, norm_bias, bucket_table = params
    branch_one = self_attention(inputs, query_weight, key_weight, value_weight, out_weight, bucket_table, reachable, distance)
    normed_one = layer_norm(inputs + branch_one, norm_gain[0], norm_bias[0])
    branch_two = cross_attention(normed_one, encoded, cross_query, cross_key, cross_value, cross_out)
    normed_two = layer_norm(normed_one + branch_two, norm_gain[1], norm_bias[1])
    branch_three = feed_forward(normed_two, expand_weight, expand_bias, reduce_weight)
    return layer_norm(normed_two + branch_three + reduce_bias, norm_gain[2], norm_bias[2])

def reference(tokens, encoded, out_cotangent, segment_start, segment_parent, query_weight, key_weight, value_weight, out_weight, cross_query, cross_key, cross_value, cross_out, expand_weight, expand_bias, reduce_weight, reduce_bias, norm_gain, norm_bias, bucket_table):
    params = (query_weight.astype(jnp.float32), key_weight.astype(jnp.float32), value_weight.astype(jnp.float32), out_weight.astype(jnp.float32), cross_query.astype(jnp.float32), cross_key.astype(jnp.float32), cross_value.astype(jnp.float32), cross_out.astype(jnp.float32), expand_weight.astype(jnp.float32), expand_bias.astype(jnp.float32), reduce_weight.astype(jnp.float32), reduce_bias.astype(jnp.float32), norm_gain.astype(jnp.float32), norm_bias.astype(jnp.float32), bucket_table.astype(jnp.float32))
    tree_rows = jnp.moveaxis(tokens.astype(jnp.float32), 1, 0)
    tree_cotangents = jnp.moveaxis(out_cotangent.astype(jnp.float32), 1, 0)
    start_grads = tuple((jnp.zeros(parameter.shape, jnp.float32) for parameter in params))

    def one_tree(carried, inputs_one):
        tree_tokens, encoder_tree, cotangent, offsets, parents = inputs_one
        reachable, distance = tree_layout(offsets, parents)

        def forward_one(tokens_in, encoded_in, param_set):
            return tree_forward(tokens_in, encoded_in, param_set, reachable, distance)
        result, pullback = jax.vjp(forward_one, tree_tokens, encoder_tree, params)
        grad_rows, grad_encoded, grad_params = pullback(cotangent)
        summed = tuple((earlier + latest for earlier, latest in zip(carried, grad_params)))
        return (summed, (result, grad_rows, grad_encoded))
    grads, (results, rows_grads, encoded_grads) = lax.scan(one_tree, start_grads, (tree_rows, encoded.astype(jnp.float32), tree_cotangents, segment_start, segment_parent))
    return (jnp.moveaxis(results, 0, 1), jnp.moveaxis(rows_grads, 0, 1), encoded_grads, grads[0], grads[1], grads[2], grads[3], grads[4], grads[5], grads[6], grads[7], grads[8], grads[9], grads[10], grads[11], grads[12], grads[13], grads[14])
```

```python
import jax
import jax.numpy as jnp
from jax import lax
from jax.sharding import PartitionSpec as P

HEAD_DIM = 64
TREE = 1024


edge_list = (16, 18, 21, 24, 27, 31, 35, 40, 45, 52, 59, 67, 76, 87, 99, 112)
norm_eps = 1e-05
masked_value = -1000000000.0
bias_block = 128
highest = lax.Precision.HIGHEST


def layer_norm(summed, gain_row, shift_row):
    center = summed - jnp.mean(summed, axis=-1, keepdims=True)
    spread = jnp.mean(center * center, axis=-1, keepdims=True)
    return center * lax.rsqrt(spread + norm_eps) * gain_row + shift_row


def gelu_exact(before):
    return jax.nn.gelu(before, approximate=False)


def tree_layout(offsets, parents):
    position = jnp.arange(TREE, dtype=jnp.int32)
    segment_count = offsets.shape[0]
    segment = jnp.sum((position[:, None] >= offsets[None, 1:]).astype(jnp.int32), axis=1)
    segment_ids = jnp.arange(segment_count, dtype=jnp.int32)
    ending = jnp.concatenate([offsets[1:], jnp.full((1,), TREE, jnp.int32)])
    segment_length = (ending - offsets).astype(jnp.float32)
    identity = (segment_ids[:, None] == segment_ids[None, :]).astype(jnp.float32)
    upward = (parents[:, None] == segment_ids[None, :]).astype(jnp.float32)
    ancestry = jnp.minimum(identity + upward + jnp.dot(upward, upward, precision=highest), 1.0)
    depth_start = jnp.dot(ancestry - identity, segment_length, precision=highest)
    token_onehot = (segment[:, None] == segment_ids[None, :]).astype(jnp.float32)
    token_start = jnp.dot(token_onehot, offsets.astype(jnp.float32), precision=highest)
    path_depth = (
        position.astype(jnp.float32)
        - token_start
        + jnp.dot(token_onehot, depth_start, precision=highest)
    )
    reach_count = jnp.dot(
        jnp.dot(token_onehot, ancestry, precision=highest), token_onehot.T, precision=highest
    )
    distance = jnp.maximum(path_depth[:, None] - path_depth[None, :], 0.0)
    return (reach_count > 0.5, distance)


def bucket_of(distance):
    crossed = jnp.zeros_like(distance)
    for edge_value in edge_list:
        crossed = crossed + (distance >= edge_value).astype(distance.dtype)
    return jnp.where(distance < 16.0, distance, 15.0 + crossed)


def bucket_onehot(block_distance, bucket_count):
    levels = jnp.arange(bucket_count, dtype=jnp.float32)
    return (bucket_of(block_distance)[:, :, None] == levels[None, None, :]).astype(jnp.float32)


def bucket_bias(distance, bucket_table):
    tree_len = distance.shape[0]
    block_rows = min(bias_block, tree_len)

    def one_block(block_distance):
        onehot = bucket_onehot(block_distance, bucket_table.shape[0])
        return jnp.einsum("qkb,bh->hqk", onehot, bucket_table, precision=highest)

    pieces = lax.map(one_block, distance.reshape(tree_len // block_rows, block_rows, distance.shape[1]))
    return jnp.moveaxis(pieces, 0, 1).reshape(bucket_table.shape[1], tree_len, distance.shape[1])


def bucket_grad(distance, score_sum, bucket_count):
    tree_len = distance.shape[0]
    block_rows = min(bias_block, tree_len)
    head_count = score_sum.shape[0]

    def one_block(block_pair):
        onehot = bucket_onehot(block_pair[0], bucket_count)
        return jnp.einsum("qkb,hqk->bh", onehot, block_pair[1], precision=highest)

    grouped = jnp.moveaxis(
        score_sum.reshape(head_count, tree_len // block_rows, block_rows, distance.shape[1]), 1, 0
    )
    blocked = distance.reshape(tree_len // block_rows, block_rows, distance.shape[1])
    return jnp.sum(lax.map(one_block, (blocked, grouped)), axis=0)


def split_heads(array_in):
    return array_in.reshape(array_in.shape[:-1] + (array_in.shape[-1] // HEAD_DIM, HEAD_DIM))


def dot_f32(spec, left, right):
    return jnp.einsum(spec, left, right, preferred_element_type=jnp.float32)


def dot_low(spec, left, right):
    return dot_f32(spec, left, right).astype(jnp.bfloat16)


def tree_rows(offsets, parents, table, first_row, row_count):
    reach_all, distance_all = tree_layout(offsets, parents)
    reachable = lax.dynamic_slice_in_dim(reach_all, first_row, row_count, 0)
    distance = lax.dynamic_slice_in_dim(distance_all, first_row, row_count, 0)
    return (reachable, distance, bucket_bias(distance, table))


def self_logits(query_heads, key_main, key_own, stream, bias_full, reachable, first_row, bucket_table):
    score_scale = HEAD_DIM ** (-0.5)
    rows = first_row + jnp.arange(query_heads.shape[0])
    columns = jnp.arange(key_main.shape[0])
    if stream == 0:
        allowed = reachable & (columns[None, :] <= rows[:, None])
    else:
        allowed = reachable & (columns[None, :] < rows[:, None])
    raw_scores = dot_f32("qhe,khe->hqk", query_heads, key_main) * score_scale
    logits = jnp.where(allowed[None], raw_scores + bias_full, masked_value)
    if stream == 0:
        return (logits, None)
    own_raw = jnp.sum(query_heads.astype(jnp.float32) * key_own.astype(jnp.float32), axis=-1)
    return (logits, own_raw.T * score_scale + bucket_table[0][:, None])


def soft_forward(logits, own_logit):
    top_value = jnp.max(logits, axis=-1)
    if own_logit is not None:
        top_value = jnp.maximum(top_value, own_logit)
    main_part = jnp.exp(logits - top_value[..., None])
    denominator = jnp.sum(main_part, axis=-1)
    own_prob = None
    if own_logit is not None:
        own_part = jnp.exp(own_logit - top_value)
        denominator = denominator + own_part
        own_prob = own_part / denominator
    return (main_part / denominator[..., None], own_prob, top_value + jnp.log(denominator))


def on_device(
    tokens,
    encoded,
    out_cotangent,
    segment_start,
    segment_parent,
    query_weight,
    key_weight,
    value_weight,
    out_weight,
    cross_query,
    cross_key,
    cross_value,
    cross_out,
    expand_weight,
    expand_bias,
    reduce_weight,
    reduce_bias,
    norm_gain,
    norm_bias,
    bucket_table,
):
    stream_count, batch_count, row_count, width = tokens.shape
    tp_index = lax.axis_index("tp")
    tp_count = lax.axis_size("tp")
    first_row = tp_index * row_count
    score_scale = HEAD_DIM ** (-0.5)

    def gather_group(*pieces):
        packed = jnp.concatenate(pieces, axis=1)[None]
        full = lax.all_gather(packed, ("tp", "fsdp"), axis=0, tiled=True)
        full = full.reshape(tp_count, width, packed.shape[2])
        bounds, low = ([], 0)
        for piece in pieces:
            bounds.append((low, low + piece.shape[1]))
            low = low + piece.shape[1]
        return tuple(
            jnp.moveaxis(full[:, :, a:b], 0, 1).reshape(width, tp_count * (b - a)) for a, b in bounds
        )

    def settle_group(*grads):
        packed = jnp.concatenate(
            [
                jnp.moveaxis(
                    grad.astype(jnp.bfloat16).reshape(width, tp_count, grad.shape[1] // tp_count), 1, 0
                )
                for grad in grads
            ],
            axis=2,
        )
        packed = lax.psum_scatter(packed, "fsdp", scatter_dimension=1, tiled=True)
        packed = lax.psum_scatter(packed, "tp", scatter_dimension=0, tiled=True)[0].astype(jnp.float32)
        settled, low = ([], 0)
        for grad in grads:
            settled.append(packed[:, low : low + grad.shape[1] // tp_count])
            low = low + grad.shape[1] // tp_count
        return settled

    main_rows = lax.all_gather(tokens[0], "tp", axis=1, tiled=True)
    w_q, w_k, w_v = gather_group(query_weight, key_weight, value_weight)
    encoder_rows = lax.all_gather(encoded, "tp", axis=1, tiled=True)
    w_ot, w_cq, w_ck, w_cv, w_cot = gather_group(
        out_weight.T, cross_query, cross_key, cross_value, cross_out.T
    )
    w_e, w_rt = gather_group(expand_weight, reduce_weight.T)
    table_full = lax.all_gather(bucket_table, "tp", axis=1, tiled=True)
    expand_full = lax.all_gather(expand_bias, "tp", axis=0, tiled=True)

    own_rows = tokens.reshape(stream_count, batch_count, row_count, width)
    query = split_heads(dot_low("sbtd,de->sbte", own_rows, w_q))
    key_main = split_heads(dot_low("btd,de->bte", main_rows, w_k))
    value_main = split_heads(dot_low("btd,de->bte", main_rows, w_v))
    key_own = split_heads(dot_low("sbtd,de->sbte", own_rows[1:], w_k))
    value_own = split_heads(dot_low("sbtd,de->sbte", own_rows[1:], w_v))
    layouts = [
        tree_rows(segment_start[b], segment_parent[b], table_full, first_row, row_count)
        for b in range(batch_count)
    ]

    def self_logits_of(stream, b):
        own = None if stream == 0 else key_own[stream - 1, b]
        return self_logits(
            query[stream, b], key_main[b], own, stream, layouts[b][2], layouts[b][0], first_row, table_full
        )

    mixed, totals = ([], {})
    for stream in range(stream_count):
        for b in range(batch_count):
            logits, own_logit = self_logits_of(stream, b)
            prob_main, own_prob, log_total = soft_forward(logits, own_logit)
            attended = dot_f32("hqk,khe->qhe", prob_main.astype(jnp.bfloat16), value_main[b])
            if own_prob is not None:
                attended = attended + own_prob.T[:, :, None] * value_own[stream - 1, b].astype(
                    jnp.float32
                )
            mixed.append(attended.reshape(row_count, width).astype(jnp.bfloat16))
            totals[stream, b] = log_total
    mixed_one = jnp.stack(mixed).reshape(own_rows.shape)
    branch_one = dot_f32("sbtk,dk->sbtd", mixed_one, w_ot)
    normed_one, pull_one = jax.vjp(
        layer_norm, own_rows.astype(jnp.float32) + branch_one, norm_gain[0], norm_bias[0]
    )
    first_low = normed_one.astype(jnp.bfloat16)
    cross_q = split_heads(dot_low("sbtd,de->sbte", first_low, w_cq))
    cross_k = split_heads(dot_low("btd,de->bte", encoder_rows, w_ck))
    cross_v = split_heads(dot_low("btd,de->bte", encoder_rows, w_cv))
    cross_logits = dot_f32("sbqhe,bkhe->sbhqk", cross_q, cross_k) * score_scale
    cross_prob, _, cross_total = soft_forward(cross_logits, None)
    mixed_two = dot_low("sbhqk,bkhe->sbqhe", cross_prob.astype(jnp.bfloat16), cross_v).reshape(
        own_rows.shape
    )
    branch_two = dot_f32("sbtk,dk->sbtd", mixed_two, w_cot)
    normed_two, pull_two = jax.vjp(
        layer_norm, normed_one + branch_two, norm_gain[1], norm_bias[1]
    )
    second_low = normed_two.astype(jnp.bfloat16)
    before = dot_f32("sbtd,df->sbtf", second_low, w_e) + expand_full
    hidden_low = gelu_exact(before).astype(jnp.bfloat16)
    branch_three = dot_f32("sbtf,df->sbtd", hidden_low, w_rt)
    layer_out, pull_three = jax.vjp(
        layer_norm, normed_two + branch_three + reduce_bias, norm_gain[2], norm_bias[2]
    )

    grad_three, gain_three, shift_three = pull_three(out_cotangent.astype(jnp.float32))
    reduce_grad = jnp.sum(grad_three, axis=(0, 1, 2))
    low_three = grad_three.astype(jnp.bfloat16)
    g_rt = dot_f32("sbtd,sbtf->df", low_three, hidden_low)
    grad_hidden = dot_f32("sbtd,df->sbtf", low_three, w_rt)
    grad_before = jax.vjp(gelu_exact, before)[1](grad_hidden)[0]
    expand_grad = jnp.sum(grad_before, axis=(0, 1, 2))
    before_low = grad_before.astype(jnp.bfloat16)
    g_e = dot_f32("sbtd,sbtf->df", second_low, before_low)
    out_e, out_rt = settle_group(g_e, g_rt)
    grad_second = grad_three + dot_f32("sbtf,df->sbtd", before_low, w_e)
    grad_two, gain_two, shift_two = pull_two(grad_second)
    low_two = grad_two.astype(jnp.bfloat16)
    g_cot = dot_f32("sbtd,sbtk->dk", low_two, mixed_two)
    grad_c = split_heads(dot_low("sbtd,dk->sbtk", low_two, w_cot))
    cross_logits = dot_f32("sbqhe,bkhe->sbhqk", cross_q, cross_k) * score_scale
    cross_prob = jnp.exp(cross_logits - cross_total[..., None])
    grad_probs = dot_f32("sbqhe,bkhe->sbhqk", grad_c, cross_v)
    inner = jnp.sum(cross_prob * grad_probs, axis=-1)
    scores_low = (cross_prob * (grad_probs - inner[..., None])).astype(jnp.bfloat16)
    d_cq = (dot_f32("sbhqk,bkhe->sbqhe", scores_low, cross_k) * score_scale).astype(jnp.bfloat16)
    d_ck = (dot_f32("sbhqk,sbqhe->bkhe", scores_low, cross_q) * score_scale).astype(jnp.bfloat16)
    d_cv = dot_low("sbhqk,sbqhe->bkhe", cross_prob.astype(jnp.bfloat16), grad_c)
    d_cq = d_cq.reshape(own_rows.shape)
    d_ck = d_ck.reshape(encoder_rows.shape)
    d_cv = d_cv.reshape(encoder_rows.shape)
    encoder_part = dot_f32("bke,de->bkd", d_ck, w_ck) + dot_f32("bke,de->bkd", d_cv, w_cv)
    encoder_grad = lax.psum_scatter(
        encoder_part.astype(jnp.bfloat16), "tp", scatter_dimension=1, tiled=True
    ).astype(jnp.float32)
    g_cq = dot_f32("sbtd,sbte->de", first_low, d_cq)
    g_ck = dot_f32("bkd,bke->de", encoder_rows, d_ck)
    g_cv = dot_f32("bkd,bke->de", encoder_rows, d_cv)
    grad_first = grad_two + dot_f32("sbte,de->sbtd", d_cq, w_cq)
    grad_one, gain_one, shift_one = pull_one(grad_first)
    low_one = grad_one.astype(jnp.bfloat16)
    g_ot = dot_f32("sbtd,sbtk->dk", low_one, mixed_one)
    out_ot, out_cq, out_ck, out_cv, out_cot = settle_group(g_ot, g_cq, g_ck, g_cv, g_cot)
    grad_a = split_heads(dot_low("sbtd,dk->sbtk", low_one, w_ot))

    query_grads, key_own_grads, value_own_grads = ({}, {}, {})
    key_mains, value_mains = ([], [])
    table_grad = jnp.zeros(table_full.shape, jnp.float32)
    first_level = (jnp.arange(table_full.shape[0]) == 0).astype(jnp.float32)
    for b in range(batch_count):
        score_sum = jnp.zeros(layouts[b][2].shape, jnp.float32)
        key_sum = jnp.zeros(key_main.shape[1:], jnp.float32)
        value_sum = jnp.zeros(value_main.shape[1:], jnp.float32)
        for stream in range(stream_count):
            logits, own_logit = self_logits_of(stream, b)
            prob_main = jnp.exp(logits - totals[stream, b][..., None])
            grad_heads = grad_a[stream, b]
            grad_probs = dot_f32("qhe,khe->hqk", grad_heads, value_main[b])
            inner = jnp.sum(prob_main * grad_probs, axis=-1)
            if own_logit is not None:
                own_prob = jnp.exp(own_logit - totals[stream, b])
                grad_own_prob = jnp.sum(
                    grad_heads.astype(jnp.float32) * value_own[stream - 1, b].astype(jnp.float32), axis=-1
                ).T
                inner = inner + own_prob * grad_own_prob
            score_grad = prob_main * (grad_probs - inner[..., None])
            score_sum = score_sum + score_grad
            scores_low = score_grad.astype(jnp.bfloat16)
            query_grad = dot_f32("hqk,khe->qhe", scores_low, key_main[b]) * score_scale
            key_sum = key_sum + dot_f32("hqk,qhe->khe", scores_low, query[stream, b]) * score_scale
            value_sum = value_sum + dot_f32(
                "hqk,qhe->khe", prob_main.astype(jnp.bfloat16), grad_heads
            )
            if own_logit is not None:
                own_grad = own_prob * (grad_own_prob - inner)
                table_grad = table_grad + first_level[:, None] * jnp.sum(own_grad, axis=1)[None, :]
                own_column = own_grad.T[:, :, None] * score_scale
                query_grad = query_grad + own_column * key_own[stream - 1, b].astype(jnp.float32)
                key_own_grads[stream, b] = own_column * query[stream, b].astype(jnp.float32)
                value_own_grads[stream, b] = own_prob.T[:, :, None] * grad_heads.astype(jnp.float32)
            query_grads[stream, b] = query_grad
        key_mains.append(key_sum)
        value_mains.append(value_sum)
        table_grad = table_grad + bucket_grad(layouts[b][1], score_sum, table_full.shape[0])

    def collect(parts, streams):
        stacked = jnp.stack([parts[s, b] for s in streams for b in range(batch_count)])
        return stacked.astype(jnp.bfloat16).reshape(len(streams), batch_count, row_count, width)

    later = list(range(1, stream_count))
    d_q = collect(query_grads, list(range(stream_count)))
    d_k_own = collect(key_own_grads, later)
    d_v_own = collect(value_own_grads, later)
    d_k_main = jnp.stack(key_mains).astype(jnp.bfloat16).reshape(main_rows.shape)
    d_v_main = jnp.stack(value_mains).astype(jnp.bfloat16).reshape(main_rows.shape)
    main_part = dot_f32("bte,de->btd", d_k_main, w_k) + dot_f32("bte,de->btd", d_v_main, w_v)
    main_grad = lax.psum_scatter(
        main_part.astype(jnp.bfloat16), "tp", scatter_dimension=1, tiled=True
    ).astype(jnp.float32)
    g_q = dot_f32("sbtd,sbte->de", own_rows, d_q)
    g_k = dot_f32("btd,bte->de", main_rows, d_k_main) + dot_f32(
        "sbtd,sbte->de", own_rows[1:], d_k_own
    )
    g_v = dot_f32("btd,bte->de", main_rows, d_v_main) + dot_f32(
        "sbtd,sbte->de", own_rows[1:], d_v_own
    )
    out_q, out_k, out_v = settle_group(g_q, g_k, g_v)
    query_part = grad_one + dot_f32("sbte,de->sbtd", d_q, w_q)
    own_part = dot_f32("sbte,de->sbtd", d_k_own, w_k) + dot_f32("sbte,de->sbtd", d_v_own, w_v)
    tokens_grad = query_part + jnp.concatenate([main_grad[None], own_part], axis=0)

    gain_total, shift_total, reduce_total, expand_total, table_total = lax.psum(
        (
            jnp.stack([gain_one, gain_two, gain_three]),
            jnp.stack([shift_one, shift_two, shift_three]),
            reduce_grad,
            expand_grad,
            table_grad,
        ),
        ("fsdp", "tp"),
    )
    expand_local = expand_bias.shape[0]
    heads_local = bucket_table.shape[1]
    return (
        layer_out,
        tokens_grad,
        encoder_grad,
        out_q,
        out_k,
        out_v,
        out_ot.T,
        out_cq,
        out_ck,
        out_cv,
        out_cot.T,
        out_e,
        lax.dynamic_slice_in_dim(expand_total, tp_index * expand_local, expand_local, 0),
        out_rt.T,
        reduce_total,
        gain_total,
        shift_total,
        lax.dynamic_slice_in_dim(table_total, tp_index * heads_local, heads_local, 1),
    )


def solution(mesh):
    placed = (
        P(None, "fsdp", "tp", None),
        P("fsdp", "tp", None),
        P(None, "fsdp", "tp", None),
        P("fsdp", None),
        P("fsdp", None),
        P("fsdp", "tp"),
        P("fsdp", "tp"),
        P("fsdp", "tp"),
        P("tp", "fsdp"),
        P("fsdp", "tp"),
        P("fsdp", "tp"),
        P("fsdp", "tp"),
        P("tp", "fsdp"),
        P("fsdp", "tp"),
        P("tp"),
        P("tp", "fsdp"),
        P(),
        P(),
        P(),
        P(None, "tp"),
    )
    return jax.shard_map(
        on_device,
        mesh=mesh,
        in_specs=placed,
        out_specs=(
            P(None, "fsdp", "tp", None),
            P(None, "fsdp", "tp", None),
            P("fsdp", "tp", None),
            P("fsdp", "tp"),
            P("fsdp", "tp"),
            P("fsdp", "tp"),
            P("tp", "fsdp"),
            P("fsdp", "tp"),
            P("fsdp", "tp"),
            P("fsdp", "tp"),
            P("tp", "fsdp"),
            P("fsdp", "tp"),
            P("tp"),
            P("tp", "fsdp"),
            P(),
            P(),
            P(),
            P(None, "tp"),
        ),
        check_vma=False,
    )
```

```python
import functools

import jax
import jax.numpy as jnp
from jax import lax
from jax.experimental import pallas as pl
from jax.experimental.pallas import tpu as pltpu
from jax.sharding import PartitionSpec as P

HEAD_DIM = 64
TREE = 1024
LANES = 128
GROUP = 4
BAND = GROUP * HEAD_DIM
MASK_SLOT = 127
edge_list = (16, 18, 21, 24, 27, 31, 35, 40, 45, 52, 59, 67, 76, 87, 99, 112)
masked_value = -1000000000.0
low_start = -1e30
score_scale = HEAD_DIM ** (-0.5)
vmem_limit = 60 * 1024 * 1024

NT = (((1,), (1,)), ((), ()))
NN = (((1,), (0,)), ((), ()))


def dot_nt(left, right):
    return lax.dot_general(left, right, NT, preferred_element_type=jnp.float32)


def dot_nn(left, right):
    return lax.dot_general(left, right, NN, preferred_element_type=jnp.float32)


def split_dot(left, right, dims):
    high = left.astype(jnp.bfloat16)
    rest = (left - high.astype(jnp.float32)).astype(jnp.bfloat16)
    return lax.dot_general(high, right, dims, preferred_element_type=jnp.float32) + lax.dot_general(
        rest, right, dims, preferred_element_type=jnp.float32
    )


def tree_facts(offsets, parents):
    count = offsets.shape[0]
    position = jnp.arange(TREE, dtype=jnp.int32)
    ids = jnp.arange(count, dtype=jnp.int32)
    segment = jnp.sum((position[:, None] >= offsets[None, 1:]).astype(jnp.int32), axis=1)
    ending = jnp.concatenate([offsets[1:], jnp.full((1,), TREE, jnp.int32)])
    length = ending - offsets

    def pick(values, index):
        return jnp.sum(jnp.where(index[:, None] == ids[None, :], values[None, :], 0), axis=1)

    grand = pick(parents, parents)
    above = jnp.where(parents == ids, 0, pick(length, parents)) + jnp.where(
        (grand == ids) | (grand == parents), 0, pick(length, grand)
    )
    base = above - offsets
    return {
        "segment": segment,
        "parent": pick(parents, segment),
        "grand": pick(grand, segment),
        "depth": position + pick(base, segment),
        "base": pick(base, segment),
        "parent_base": pick(pick(base, parents), segment),
        "grand_base": pick(pick(base, grand), segment),
        "start_depth": pick(above, segment),
        "parent_depth": pick(pick(above, parents), segment),
        "position": position,
    }


def tree_index(facts, block, row_count):
    tiles = TREE // row_count

    def one_block(value, which):
        return lax.dynamic_slice_in_dim(value, which * row_count, row_count, 0)

    order = [lax.rem(block - k + tiles, tiles) for k in range(tiles)]
    own = {name: one_block(value, block) for name, value in facts.items()}
    facts = {
        name: jnp.concatenate([one_block(value, which) for which in order]) for name, value in facts.items()
    }

    def slots(row, key):
        reach = (
            (key("segment") == row("segment"))
            | (key("segment") == row("parent"))
            | (key("segment") == row("grand"))
        ) & (key("position") <= row("position"))
        distance = jnp.maximum(row("depth") - key("depth"), 0)
        crossed = jnp.zeros_like(distance)
        for edge in edge_list:
            crossed = crossed + (distance >= edge).astype(jnp.int32)
        bucket = jnp.where(distance < 16, distance, 15 + crossed)
        return jnp.where(reach, bucket, MASK_SLOT)

    by_row = slots(lambda n: own[n][:, None], lambda n: facts[n][None, :])
    by_key = slots(lambda n: own[n][None, :], lambda n: facts[n][:, None])
    back = jnp.arange(LANES, dtype=jnp.int32)[None, :]
    target = own["depth"][:, None] - back
    place = jnp.where(
        target >= own["start_depth"][:, None],
        target - own["base"][:, None],
        jnp.where(
            target >= own["parent_depth"][:, None],
            target - own["parent_base"][:, None],
            target - own["grand_base"][:, None],
        ),
    )
    place = lax.rem(block - place // row_count + tiles, tiles) * row_count + lax.rem(place, row_count)
    near = jnp.where((target >= 0) & (back < edge_list[-1]), place, -1)
    return (by_row, by_key, near)


def head_lanes(rows, head):
    lane = lax.broadcasted_iota(jnp.int32, (rows, BAND), 1)
    return lane // HEAD_DIM == head


def self_forward_kernel(
    flag_ref, q_ref, k_ref, v_ref, ki_ref, vi_ref, idx_ref, table_ref, zero_ref,
    att_ref, lse_ref, qm_ref, m_ref, l_ref, acc_ref,
):
    b, g, kt = pl.program_id(0), pl.program_id(1), pl.program_id(2)
    streams, rows = q_ref.shape[0], q_ref.shape[2]
    keys = k_ref.shape[2]

    @pl.when(kt == 0)
    def _():
        lane = lax.broadcasted_iota(jnp.int32, (8, BAND), 1) // HEAD_DIM
        pick = (lane == lax.broadcasted_iota(jnp.int32, (8, BAND), 0)).astype(jnp.bfloat16)
        for s in range(streams):
            for h in range(GROUP):
                qm_ref[h * streams + s] = jnp.where(
                    head_lanes(rows, h), q_ref[s, 0] * jnp.bfloat16(score_scale), jnp.bfloat16(0)
                )
            if s > 0:
                own = q_ref[s, 0].astype(jnp.float32) * ki_ref[s - 1, 0].astype(jnp.float32) * score_scale
                high = own.astype(jnp.bfloat16)
                rest = (own - high.astype(jnp.float32)).astype(jnp.bfloat16)
                logit = dot_nt(pick, high) + dot_nt(pick, rest) + zero_ref[0, :, 0:1]
                value_t = vi_ref[s - 1, 0].astype(jnp.float32).T
            for h in range(GROUP):
                n = h * streams + s
                if s > 0:
                    m_ref[n : n + 1, :] = logit[h : h + 1, :]
                    l_ref[n : n + 1, :] = jnp.ones((1, rows), jnp.float32)
                    acc_ref[n] = value_t[h * HEAD_DIM : (h + 1) * HEAD_DIM, :]
                else:
                    m_ref[n : n + 1, :] = jnp.full((1, rows), low_start, jnp.float32)
                    l_ref[n : n + 1, :] = jnp.zeros((1, rows), jnp.float32)
                    acc_ref[n] = jnp.zeros((HEAD_DIM, rows), jnp.float32)

    @pl.when(flag_ref[b, kt] > 0)
    def _():
        value_t = v_ref[0, 0].astype(jnp.float32).T.astype(jnp.bfloat16)
        same = lax.broadcasted_iota(jnp.int32, (keys, rows), 0) == lax.broadcasted_iota(
            jnp.int32, (keys, rows), 1
        )
        diagonal = same & (kt == 0)
        for h in range(GROUP):
            line = jnp.broadcast_to(table_ref[0, h : h + 1, :], (keys, LANES))
            bias = jnp.concatenate(
                [
                    jnp.take_along_axis(line, idx_ref[0, :, c * LANES : (c + 1) * LANES], axis=1)
                    for c in range(rows // LANES)
                ],
                axis=1,
            )
            for s in range(streams):
                n = h * streams + s
                logits = dot_nt(k_ref[0, 0], qm_ref[n]) + bias
                if s > 0:
                    logits = jnp.where(diagonal, masked_value, logits)
                old = m_ref[n : n + 1, :]
                top = jnp.maximum(old, jnp.max(logits, axis=0, keepdims=True))
                fade = jnp.exp(old - top)
                part = jnp.exp(logits - top)
                m_ref[n : n + 1, :] = top
                l_ref[n : n + 1, :] = l_ref[n : n + 1, :] * fade + jnp.sum(part, axis=0, keepdims=True)
                acc_ref[n] = acc_ref[n] * fade + dot_nn(
                    value_t[h * HEAD_DIM : (h + 1) * HEAD_DIM, :], part.astype(jnp.bfloat16)
                )

    @pl.when(kt == pl.num_programs(2) - 1)
    def _():
        lse_ref[0, 0] = jnp.zeros(lse_ref.shape[2:], jnp.float32)
        for s in range(streams):
            pieces = []
            for h in range(GROUP):
                n = h * streams + s
                total = l_ref[n : n + 1, :]
                pieces.append(acc_ref[n] / total)
                lse_ref[0, 0, s * 8 + h : s * 8 + h + 1, :] = m_ref[n : n + 1, :] + jnp.log(total)
            att_ref[s, 0] = jnp.concatenate(pieces, axis=0).T.astype(jnp.bfloat16)


def self_forward(flags, query, key_main, value_main, key_own, value_own, by_key, table, zero):
    streams, batch, rows, width = query.shape
    groups = width // BAND
    tiles = key_main.shape[0]
    own = lambda b, g, k, *_: (0, b, 0, g)
    main = lambda b, g, k, *_: (k, b, 0, g)
    return pl.pallas_call(
        self_forward_kernel,
        out_shape=(
            jax.ShapeDtypeStruct(query.shape, jnp.bfloat16),
            jax.ShapeDtypeStruct((batch, groups, streams * 8, rows), jnp.float32),
        ),
        grid_spec=pltpu.PrefetchScalarGridSpec(
            num_scalar_prefetch=1,
            grid=(batch, groups, tiles),
            in_specs=[
                pl.BlockSpec((streams, 1, rows, BAND), own),
                pl.BlockSpec((1, 1, rows, BAND), main),
                pl.BlockSpec((1, 1, rows, BAND), main),
                pl.BlockSpec((streams - 1, 1, rows, BAND), own),
                pl.BlockSpec((streams - 1, 1, rows, BAND), own),
                pl.BlockSpec((1, rows, rows), lambda b, g, k, *_: (b, k, 0)),
                pl.BlockSpec((1, 8, LANES), lambda b, g, k, *_: (g, 0, 0)),
                pl.BlockSpec((1, 8, LANES), lambda b, g, k, *_: (g, 0, 0)),
            ],
            out_specs=[
                pl.BlockSpec((streams, 1, rows, BAND), own),
                pl.BlockSpec((1, 1, streams * 8, rows), lambda b, g, k, *_: (b, g, 0, 0)),
            ],
            scratch_shapes=[
                pltpu.VMEM((GROUP * streams, rows, BAND), jnp.bfloat16),
                pltpu.VMEM((16, rows), jnp.float32),
                pltpu.VMEM((16, rows), jnp.float32),
                pltpu.VMEM((GROUP * streams, HEAD_DIM, rows), jnp.float32),
            ],
        ),
        compiler_params=pltpu.CompilerParams(vmem_limit_bytes=vmem_limit),
        cost_estimate=cost(16 * streams * batch * rows * tiles * rows * width, 8 * query.size + 8 * key_main.size),
        name="self_forward",
    )(flags, query, key_main, value_main, key_own, value_own, by_key, table, zero)


def self_backward_kernel(
    flag_ref, q_ref, k_ref, v_ref, ki_ref, vi_ref, do_ref, att_ref, lse_ref, idx_ref,
    near_ref, table_ref, zero_ref,
    dq_ref, dk_ref, dv_ref, dki_ref, dvi_ref, hist_ref, total_ref, own_ref,
    qm_ref, dom_ref, qt_ref, dot_ref, lse_col, delta_col, acc_ref, p_all, ds_all,
):
    b, g, kt = pl.program_id(0), pl.program_id(1), pl.program_id(2)
    streams, rows = q_ref.shape[0], q_ref.shape[2]
    keys = k_ref.shape[2]
    scale = jnp.bfloat16(score_scale)

    @pl.when(kt == 0)
    def _():
        pick = (
            lax.broadcasted_iota(jnp.int32, (BAND, LANES), 0) // HEAD_DIM
            == lax.broadcasted_iota(jnp.int32, (BAND, LANES), 1)
        ).astype(jnp.bfloat16)
        lane_ok = lax.broadcasted_iota(jnp.int32, (rows, LANES), 1) < GROUP
        lse_all = lse_ref[0, 0].T
        own_sum = jnp.zeros((8, LANES), jnp.float32)
        for s in range(streams):
            span = slice(s * rows, (s + 1) * rows)
            q, do = q_ref[s, 0], do_ref[s, 0]
            q32, do32 = q.astype(jnp.float32), do.astype(jnp.float32)
            delta = split_dot(do32 * att_ref[s, 0].astype(jnp.float32), pick, NN)
            for h in range(GROUP):
                inside = head_lanes(rows, h)
                qm_ref[h, span, :] = jnp.where(inside, q * scale, jnp.bfloat16(0))
                dom_ref[h, span, :] = jnp.where(inside, do, jnp.bfloat16(0))
                delta_col[h, span, :] = jnp.broadcast_to(delta[:, h : h + 1], (rows, LANES))
                lse_col[h, span, :] = jnp.broadcast_to(
                    lse_all[:, s * 8 + h : s * 8 + h + 1], (rows, LANES)
                )
            qt_ref[:, span] = (q32 * score_scale).T.astype(jnp.bfloat16)
            dot_ref[:, span] = do32.T.astype(jnp.bfloat16)
            if s == 0:
                acc_ref[span, :] = jnp.zeros((rows, BAND), jnp.float32)
                continue
            ki32 = ki_ref[s - 1, 0].astype(jnp.float32)
            vi32 = vi_ref[s - 1, 0].astype(jnp.float32)
            logit = split_dot(q32 * ki32 * score_scale, pick, NN) + zero_ref[0, 0:1, :]
            lse_here = jnp.concatenate(
                [lse_all[:, s * 8 : s * 8 + 8], jnp.zeros((rows, LANES - 8), jnp.float32)], axis=1
            )
            prob = jnp.where(lane_ok, jnp.exp(jnp.where(lane_ok, logit - lse_here, 0.0)), 0.0)
            grad = prob * (split_dot(do32 * vi32, pick, NN) - delta)
            own_sum = own_sum + jnp.sum(grad.reshape(rows // 8, 8, LANES), axis=0)
            grad_full = split_dot(grad, pick, NT)
            prob_full = split_dot(prob, pick, NT)
            dki_ref[s - 1, 0] = (grad_full * q32 * score_scale).astype(jnp.bfloat16)
            dvi_ref[s - 1, 0] = (prob_full * do32).astype(jnp.bfloat16)
            acc_ref[span, :] = grad_full * ki32 * score_scale
        own_ref[0, 0] = own_sum
        hist_ref[0, 0] = jnp.zeros(hist_ref.shape[2:], jnp.float32)
        total_ref[0, 0] = jnp.zeros(total_ref.shape[2:], jnp.float32)

    @pl.when(flag_ref[b, kt] == 0)
    def _():
        dk_ref[0, 0] = jnp.zeros((keys, BAND), jnp.bfloat16)
        dv_ref[0, 0] = jnp.zeros((keys, BAND), jnp.bfloat16)

    @pl.when(flag_ref[b, kt] > 0)
    def _():
        same = lax.broadcasted_iota(jnp.int32, (rows, keys), 0) == lax.broadcasted_iota(
            jnp.int32, (rows, keys), 1
        )
        diagonal = same & (kt == 0)
        dk_parts, dv_parts = [], []
        for h in range(GROUP):
            line = jnp.broadcast_to(table_ref[0, h : h + 1, :], (rows, LANES))
            bias = jnp.concatenate(
                [
                    jnp.take_along_axis(line, idx_ref[0, :, c * LANES : (c + 1) * LANES], axis=1)
                    for c in range(keys // LANES)
                ],
                axis=1,
            )
            score_sum = None
            for s in range(streams):
                span = slice(s * rows, (s + 1) * rows)
                shift = jnp.concatenate([lse_col[h, span, :]] * (keys // LANES), axis=1)
                delta = jnp.concatenate([delta_col[h, span, :]] * (keys // LANES), axis=1)
                prob = jnp.exp(dot_nt(qm_ref[h, span, :], k_ref[0, 0]) + bias - shift)
                if s > 0:
                    prob = jnp.where(diagonal, 0.0, prob)
                grad = prob * (dot_nt(dom_ref[h, span, :], v_ref[0, 0]) - delta)
                score_sum = grad if s == 0 else score_sum + grad
                p_all[span, h * keys : (h + 1) * keys] = prob.astype(jnp.bfloat16)
                ds_all[span, h * keys : (h + 1) * keys] = grad.astype(jnp.bfloat16)
            total_ref[0, 0, h] += sum(
                jnp.sum(
                    score_sum[:, c * LANES : (c + 1) * LANES].reshape(rows // 8, 8, LANES), axis=0
                )
                for c in range(keys // LANES)
            )

            near = None
            for c in range(keys // LANES):
                place = near_ref[0] - (kt * keys + c * LANES)
                inside = (place >= 0) & (place < LANES)
                taken = jnp.take_along_axis(
                    score_sum[:, c * LANES : (c + 1) * LANES], jnp.clip(place, 0, LANES - 1), axis=1
                )
                taken = jnp.where(inside, taken, 0.0)
                near = taken if c == 0 else near + taken
            hist_ref[0, 0, h] += jnp.sum(near.reshape(rows // 8, 8, LANES), axis=0)
            lines = slice(h * HEAD_DIM, (h + 1) * HEAD_DIM)
            dk_parts.append(dot_nn(qt_ref[lines, :], ds_all[:, h * keys : (h + 1) * keys]))
            dv_parts.append(dot_nn(dot_ref[lines, :], p_all[:, h * keys : (h + 1) * keys]))
        dk_ref[0, 0] = jnp.concatenate(dk_parts, axis=0).T.astype(jnp.bfloat16)
        dv_ref[0, 0] = jnp.concatenate(dv_parts, axis=0).T.astype(jnp.bfloat16)
        masked_keys = jnp.concatenate(
            [jnp.where(head_lanes(keys, h), k_ref[0, 0] * scale, jnp.bfloat16(0)) for h in range(GROUP)],
            axis=0,
        )
        acc_ref[...] += dot_nn(ds_all[...], masked_keys)

    @pl.when(kt == pl.num_programs(2) - 1)
    def _():
        for s in range(streams):
            dq_ref[s, 0] = acc_ref[s * rows : (s + 1) * rows, :].astype(jnp.bfloat16)


def self_backward(
    flags, query, key_main, value_main, key_own, value_own, grad_a, attended, lse, by_row, near,
    table, zero,
):
    streams, batch, rows, width = query.shape
    groups = width // BAND
    tiles = key_main.shape[0]
    own = lambda b, g, k, *_: (0, b, 0, g)
    main = lambda b, g, k, *_: (k, b, 0, g)
    full = lambda b, g, k, *_: (b, g, 0, 0)
    hist = lambda b, g, k, *_: (b, g, 0, 0, 0)
    own_block = pl.BlockSpec((streams, 1, rows, BAND), own)
    later_block = pl.BlockSpec((streams - 1, 1, rows, BAND), own)
    main_block = pl.BlockSpec((1, 1, rows, BAND), main)
    hist_shape = jax.ShapeDtypeStruct((batch, groups, GROUP, 8, LANES), jnp.float32)
    hist_block = pl.BlockSpec((1, 1, GROUP, 8, LANES), hist)
    return pl.pallas_call(
        self_backward_kernel,
        out_shape=(
            jax.ShapeDtypeStruct(query.shape, jnp.bfloat16),
            jax.ShapeDtypeStruct(key_main.shape, jnp.bfloat16),
            jax.ShapeDtypeStruct(key_main.shape, jnp.bfloat16),
            jax.ShapeDtypeStruct(key_own.shape, jnp.bfloat16),
            jax.ShapeDtypeStruct(key_own.shape, jnp.bfloat16),
            hist_shape,
            hist_shape,
            jax.ShapeDtypeStruct((batch, groups, 8, LANES), jnp.float32),
        ),
        grid_spec=pltpu.PrefetchScalarGridSpec(
            num_scalar_prefetch=1,
            grid=(batch, groups, tiles),
            in_specs=[
                own_block, main_block, main_block, later_block, later_block, own_block, own_block,
                pl.BlockSpec((1, 1, streams * 8, rows), full),
                pl.BlockSpec((1, rows, rows), lambda b, g, k, *_: (b, 0, k)),
                pl.BlockSpec((1, rows, LANES), lambda b, g, k, *_: (b, 0, 0)),
                pl.BlockSpec((1, 8, LANES), lambda b, g, k, *_: (g, 0, 0)),
                pl.BlockSpec((1, 8, LANES), lambda b, g, k, *_: (g, 0, 0)),
            ],
            out_specs=[
                own_block, main_block, main_block, later_block, later_block, hist_block, hist_block,
                pl.BlockSpec((1, 1, 8, LANES), full),
            ],
            scratch_shapes=[
                pltpu.VMEM((GROUP, streams * rows, BAND), jnp.bfloat16),
                pltpu.VMEM((GROUP, streams * rows, BAND), jnp.bfloat16),
                pltpu.VMEM((BAND, streams * rows), jnp.bfloat16),
                pltpu.VMEM((BAND, streams * rows), jnp.bfloat16),
                pltpu.VMEM((GROUP, streams * rows, LANES), jnp.float32),
                pltpu.VMEM((GROUP, streams * rows, LANES), jnp.float32),
                pltpu.VMEM((streams * rows, BAND), jnp.float32),
                pltpu.VMEM((streams * rows, GROUP * rows), jnp.bfloat16),
                pltpu.VMEM((streams * rows, GROUP * rows), jnp.bfloat16),
            ],
        ),
        compiler_params=pltpu.CompilerParams(vmem_limit_bytes=vmem_limit),
        cost_estimate=cost(40 * streams * batch * rows * tiles * rows * width, 12 * query.size + 12 * key_main.size),
        name="self_backward",
    )(
        flags, query, key_main, value_main, key_own, value_own, grad_a, attended, lse, by_row, near,
        table, zero,
    )


def join_keys(ref):
    return ref[:, 0].reshape(ref.shape[0] * ref.shape[2], BAND)


def cross_forward_kernel(q_ref, k_ref, v_ref, att_ref, lse_ref):
    streams, rows = q_ref.shape[0], q_ref.shape[2]
    key, value = join_keys(k_ref), join_keys(v_ref)
    value_t = value.astype(jnp.float32).T.astype(jnp.bfloat16)
    lse_ref[0, 0] = jnp.zeros(lse_ref.shape[2:], jnp.float32)
    for s in range(streams):
        pieces = []
        for h in range(GROUP):
            masked = jnp.where(
                head_lanes(rows, h), q_ref[s, 0] * jnp.bfloat16(score_scale), jnp.bfloat16(0)
            )
            logits = dot_nt(key, masked)
            top = jnp.max(logits, axis=0, keepdims=True)
            part = jnp.exp(logits - top)
            total = jnp.sum(part, axis=0, keepdims=True)
            lse_ref[0, 0, s * 8 + h : s * 8 + h + 1, :] = top + jnp.log(total)
            mixed = dot_nn(value_t[h * HEAD_DIM : (h + 1) * HEAD_DIM, :], part.astype(jnp.bfloat16))
            pieces.append(mixed / total)
        att_ref[s, 0] = jnp.concatenate(pieces, axis=0).T.astype(jnp.bfloat16)


def cross_forward(query, key, value):
    streams, batch, rows, width = query.shape
    groups, keys = width // BAND, key.shape[0] * key.shape[2]
    own_block = pl.BlockSpec((streams, 1, rows, BAND), lambda b, g: (0, b, 0, g))
    key_block = pl.BlockSpec((key.shape[0], 1, key.shape[2], BAND), lambda b, g: (0, b, 0, g))
    return pl.pallas_call(
        cross_forward_kernel,
        out_shape=(
            jax.ShapeDtypeStruct(query.shape, jnp.bfloat16),
            jax.ShapeDtypeStruct((batch, groups, streams * 8, rows), jnp.float32),
        ),
        grid=(batch, groups),
        in_specs=[own_block, key_block, key_block],
        out_specs=[own_block, pl.BlockSpec((1, 1, streams * 8, rows), lambda b, g: (b, g, 0, 0))],
        compiler_params=pltpu.CompilerParams(vmem_limit_bytes=vmem_limit),
        cost_estimate=cost(16 * streams * batch * rows * keys * width, 6 * query.size + 4 * key.size),
        name="cross_forward",
    )(query, key, value)


def cross_backward_kernel(
    q_ref, k_ref, v_ref, do_ref, att_ref, lse_ref, dq_ref, dk_ref, dv_ref, p_all, ds_all
):
    streams, rows = q_ref.shape[0], q_ref.shape[2]
    key, value = join_keys(k_ref), join_keys(v_ref)
    keys = key.shape[0]
    scale = jnp.bfloat16(score_scale)
    pick = (
        lax.broadcasted_iota(jnp.int32, (BAND, LANES), 0) // HEAD_DIM
        == lax.broadcasted_iota(jnp.int32, (BAND, LANES), 1)
    ).astype(jnp.bfloat16)
    lse_all = lse_ref[0, 0].T
    query_t, grad_t = [], []
    for s in range(streams):
        span = slice(s * rows, (s + 1) * rows)
        q, do = q_ref[s, 0], do_ref[s, 0]
        do32 = do.astype(jnp.float32)
        delta = split_dot(do32 * att_ref[s, 0].astype(jnp.float32), pick, NN)
        query_t.append((q.astype(jnp.float32) * score_scale).T.astype(jnp.bfloat16))
        grad_t.append(do32.T.astype(jnp.bfloat16))
        for h in range(GROUP):
            inside = head_lanes(rows, h)
            logits = dot_nt(jnp.where(inside, q * scale, jnp.bfloat16(0)), key)
            prob = jnp.exp(logits - lse_all[:, s * 8 + h : s * 8 + h + 1])
            grad = dot_nt(jnp.where(inside, do, jnp.bfloat16(0)), value)
            grad = prob * (grad - delta[:, h : h + 1])
            p_all[span, h * keys : (h + 1) * keys] = prob.astype(jnp.bfloat16)
            ds_all[span, h * keys : (h + 1) * keys] = grad.astype(jnp.bfloat16)
    query_t = jnp.concatenate(query_t, axis=1)
    grad_t = jnp.concatenate(grad_t, axis=1)
    dk_parts, dv_parts = [], []
    for h in range(GROUP):
        lines = slice(h * HEAD_DIM, (h + 1) * HEAD_DIM)
        dk_parts.append(dot_nn(query_t[lines, :], ds_all[:, h * keys : (h + 1) * keys]))
        dv_parts.append(dot_nn(grad_t[lines, :], p_all[:, h * keys : (h + 1) * keys]))
    dk_ref[:, 0] = jnp.concatenate(dk_parts, axis=0).T.astype(jnp.bfloat16).reshape(dk_ref.shape[0], -1, BAND)
    dv_ref[:, 0] = jnp.concatenate(dv_parts, axis=0).T.astype(jnp.bfloat16).reshape(dv_ref.shape[0], -1, BAND)
    masked_keys = jnp.concatenate(
        [jnp.where(head_lanes(keys, h), key * scale, jnp.bfloat16(0)) for h in range(GROUP)],
        axis=0,
    )
    for s in range(streams):
        span = slice(s * rows, (s + 1) * rows)
        dq_ref[s, 0] = dot_nn(ds_all[span, :], masked_keys).astype(jnp.bfloat16)


def cross_backward(query, key, value, grad_c, attended, lse):
    streams, batch, rows, width = query.shape
    groups, keys = width // BAND, key.shape[0] * key.shape[2]
    own_block = pl.BlockSpec((streams, 1, rows, BAND), lambda b, g: (0, b, 0, g))
    key_block = pl.BlockSpec((key.shape[0], 1, key.shape[2], BAND), lambda b, g: (0, b, 0, g))
    return pl.pallas_call(
        cross_backward_kernel,
        out_shape=(
            jax.ShapeDtypeStruct(query.shape, jnp.bfloat16),
            jax.ShapeDtypeStruct(key.shape, jnp.bfloat16),
            jax.ShapeDtypeStruct(key.shape, jnp.bfloat16),
        ),
        grid=(batch, groups),
        in_specs=[
            own_block, key_block, key_block, own_block, own_block,
            pl.BlockSpec((1, 1, streams * 8, rows), lambda b, g: (b, g, 0, 0)),
        ],
        out_specs=[own_block, key_block, key_block],
        scratch_shapes=[
            pltpu.VMEM((streams * rows, GROUP * keys), jnp.bfloat16),
            pltpu.VMEM((streams * rows, GROUP * keys), jnp.bfloat16),
        ],
        compiler_params=pltpu.CompilerParams(vmem_limit_bytes=vmem_limit),
        cost_estimate=cost(40 * streams * batch * rows * keys * width, 12 * query.size + 8 * key.size),
        name="cross_backward",
    )(query, key, value, grad_c, attended, lse)


ROWS = 256
cost_part = 16
norm_eps = 1e-05
inv_root_two = 0.7071067811865476
density_scale = 0.3989422804014327


def whole(shape, buffers=1):
    return pl.BlockSpec(shape, lambda *_: (0,) * len(shape), pipeline_mode=pl.Buffered(buffers))


def params(**extra):
    return pltpu.CompilerParams(vmem_limit_bytes=vmem_limit, **extra)


def cost(flops, size):
    return pl.CostEstimate(
        flops=int(flops) // cost_part, bytes_accessed=int(size) // cost_part, transcendentals=0
    )


def project_kernel(count, skip, x_count, *refs):
    xs, rest = refs[:x_count], refs[x_count:]
    for n in range(count):
        at = 0
        for x_ref in xs:
            rows = x_ref.shape[0] - skip[n]
            rest[count + n][at : at + rows, :] = dot_nn(x_ref[skip[n] :, :], rest[n][0]).astype(jnp.bfloat16)
            at += rows


def project(pieces, weights, skip):
    count = len(weights)
    height = sum(piece.shape[0] for piece in pieces)
    width = pieces[0].shape[1]
    parts = weights[0].shape[0]
    return pl.pallas_call(
        functools.partial(project_kernel, count, skip, len(pieces)),
        out_shape=tuple(jax.ShapeDtypeStruct((height - s, width), jnp.bfloat16) for s in skip),
        grid=(parts,),
        in_specs=[whole(piece.shape) for piece in pieces]
        + [pl.BlockSpec((1, width, BAND), lambda p: (p, 0, 0))] * count,
        out_specs=[pl.BlockSpec((height - s, BAND), lambda p: (0, p)) for s in skip],
        compiler_params=params(),
        cost_estimate=cost(2 * height * width * width * count, 4 * height * width * count),
        name="project",
    )(*pieces, *weights)


def sum_bands_nt(left, packed_ref):
    total = dot_nt(left[:, 0:BAND], packed_ref[0])
    for p in range(1, packed_ref.shape[0]):
        total = total + dot_nt(left[:, p * BAND : (p + 1) * BAND], packed_ref[p])
    return total


def normalize(summed):
    center = summed - jnp.mean(summed, axis=-1, keepdims=True)
    spread = jnp.mean(center * center, axis=-1, keepdims=True)
    scale = lax.rsqrt(spread + norm_eps)
    return center * scale, scale


def norm_back(grad, hat, scale, gain):
    inner = grad * gain
    return scale * (
        inner
        - jnp.mean(inner, axis=-1, keepdims=True)
        - hat * jnp.mean(inner * hat, axis=-1, keepdims=True)
    )


def fold(values):
    return jnp.sum(values.reshape(values.shape[0] // 8, 8, values.shape[1]), axis=0)


def first_norm_kernel(mix_ref, tok_ref, wo_ref, wq_ref, gain_ref, shift_ref, hat_ref, scale_ref, low_ref, q_ref):
    summed = tok_ref[...].astype(jnp.float32) + sum_bands_nt(mix_ref[...], wo_ref)
    hat, scale = normalize(summed)
    hat_ref[...] = hat.astype(jnp.bfloat16)
    scale_ref[...] = jnp.broadcast_to(scale, scale_ref.shape)
    low = (hat * gain_ref[0:1, :] + shift_ref[0:1, :]).astype(jnp.bfloat16)
    low_ref[...] = low
    for p in range(wq_ref.shape[0]):
        q_ref[:, p * BAND : (p + 1) * BAND] = dot_nn(low, wq_ref[p]).astype(jnp.bfloat16)


def first_norm(mixed, tokens, w_out, w_query, gain, shift):
    height, width = tokens.shape
    tile = pl.BlockSpec((ROWS, width), lambda i: (i, 0))
    low = jax.ShapeDtypeStruct((height, width), jnp.bfloat16)
    return pl.pallas_call(
        first_norm_kernel,
        out_shape=(low, jax.ShapeDtypeStruct((height, LANES), jnp.float32), low, low),
        grid=(height // ROWS,),
        in_specs=[
            tile, tile, whole(w_out.shape), whole(w_query.shape), whole(gain.shape), whole(shift.shape)
        ],
        out_specs=[tile, pl.BlockSpec((ROWS, LANES), lambda i: (i, 0)), tile, tile],
        compiler_params=params(),
        cost_estimate=cost(4 * height * width * width, 12 * height * width),
        name="first_norm",
    )(mixed, tokens, w_out, w_query, gain, shift)


def feed_kernel(
    mix_ref, hat_ref, cot_ref, wo_ref, wf_ref, gain_ref, shift_ref, ebias_ref, rbias_ref,
    out_ref, low_ref, hid_ref, du_ref, d3_ref, d2_ref, dz2_ref, dc_ref, sums_ref, esum_ref, slope_ref,
):
    parts, width = wf_ref.shape[0], wf_ref.shape[1]
    hidden = wf_ref.shape[2] // 2
    step = 512

    @pl.when(pl.program_id(0) == 0)
    def _():
        sums_ref[...] = jnp.zeros_like(sums_ref)
        esum_ref[...] = jnp.zeros_like(esum_ref)

    first = hat_ref[...].astype(jnp.float32) * gain_ref[0:1, :] + shift_ref[0:1, :]
    hat2, scale2 = normalize(first + sum_bands_nt(mix_ref[...], wo_ref))
    second = hat2 * gain_ref[1:2, :] + shift_ref[1:2, :]
    low = second.astype(jnp.bfloat16)
    low_ref[...] = low
    y3 = second + rbias_ref[...]
    for p in range(parts):
        for c in range(0, hidden, step):
            at = p * hidden + c
            u = dot_nn(low, wf_ref[p, :, c : c + step]) + ebias_ref[:, at : at + step]
            half = 0.5 + 0.5 * lax.erf(u * inv_root_two)
            slope_ref[:, at : at + step] = (half + u * (density_scale * jnp.exp(-0.5 * u * u))).astype(
                jnp.bfloat16
            )
            hid = (u * half).astype(jnp.bfloat16)
            hid_ref[:, at : at + step] = hid
            y3 = y3 + dot_nt(hid, wf_ref[p, :, hidden + c : hidden + c + step])
    hat3, scale3 = normalize(y3)
    out_ref[...] = hat3 * gain_ref[2:3, :] + shift_ref[2:3, :]
    cot = cot_ref[...].astype(jnp.float32)
    sums_ref[0] += fold(cot * hat3)
    sums_ref[1] += fold(cot)
    dz3 = norm_back(cot, hat3, scale3, gain_ref[2:3, :])
    sums_ref[2] += fold(dz3)
    d3 = dz3.astype(jnp.bfloat16)
    d3_ref[...] = d3
    back = dz3
    for p in range(parts):
        for c in range(0, hidden, step):
            at = p * hidden + c
            du = dot_nn(d3, wf_ref[p, :, hidden + c : hidden + c + step]) * slope_ref[
                :, at : at + step
            ].astype(jnp.float32)
            esum_ref[:, at : at + step] += fold(du)
            du_low = du.astype(jnp.bfloat16)
            du_ref[:, at : at + step] = du_low
            back = back + dot_nt(du_low, wf_ref[p, :, c : c + step])
    sums_ref[3] += fold(back * hat2)
    sums_ref[4] += fold(back)
    dz2 = norm_back(back, hat2, scale2, gain_ref[1:2, :])
    dz2_ref[...] = dz2
    d2 = dz2.astype(jnp.bfloat16)
    d2_ref[...] = d2
    for p in range(parts):
        dc_ref[:, p * BAND : (p + 1) * BAND] = dot_nn(d2, wo_ref[p]).astype(jnp.bfloat16)


def feed(mixed, hat, cotangent, w_out, feed_packed, gain, shift, expand_bias, reduce_bias):
    height, width = mixed.shape
    parts, _, double = feed_packed.shape
    total = parts * double // 2
    tile = pl.BlockSpec((ROWS, width), lambda i: (i, 0))
    wide = pl.BlockSpec((ROWS, total), lambda i: (i, 0))
    low = jax.ShapeDtypeStruct((height, width), jnp.bfloat16)
    low_wide = jax.ShapeDtypeStruct((height, total), jnp.bfloat16)
    full = jax.ShapeDtypeStruct((height, width), jnp.float32)
    return pl.pallas_call(
        feed_kernel,
        out_shape=(
            full, low, low_wide, low_wide, low, low, full, low,
            jax.ShapeDtypeStruct((5, 8, width), jnp.float32),
            jax.ShapeDtypeStruct((8, total), jnp.float32),
        ),
        grid=(height // ROWS,),
        in_specs=[
            tile, tile, tile, whole(w_out.shape), whole(feed_packed.shape), whole(gain.shape),
            whole(shift.shape), whole((1, total)), whole((1, width)),
        ],
        out_specs=[
            tile, tile, wide, wide, tile, tile, tile, tile,
            pl.BlockSpec((5, 8, width), lambda i: (0, 0, 0)),
            pl.BlockSpec((8, total), lambda i: (0, 0)),
        ],
        scratch_shapes=[pltpu.VMEM((ROWS, total), jnp.bfloat16)],
        compiler_params=params(),
        cost_estimate=cost(8 * height * width * total + 4 * height * width * width, 40 * height * width),
        name="feed",
    )(mixed, hat, cotangent, w_out, feed_packed, gain, shift, expand_bias[None], reduce_bias[None])


def first_back_kernel(dq_ref, dz2_ref, hat_ref, scale_ref, wq_ref, wo_ref, gain_ref, dz1_ref, d1_ref, da_ref, sums_ref):
    @pl.when(pl.program_id(0) == 0)
    def _():
        sums_ref[...] = jnp.zeros_like(sums_ref)

    grad = dz2_ref[...] + sum_bands_nt(dq_ref[...], wq_ref)
    hat = hat_ref[...].astype(jnp.float32)
    sums_ref[0] += fold(grad * hat)
    sums_ref[1] += fold(grad)
    dz1 = norm_back(grad, hat, scale_ref[:, 0:1], gain_ref[0:1, :])
    dz1_ref[...] = dz1
    d1 = dz1.astype(jnp.bfloat16)
    d1_ref[...] = d1
    for p in range(wo_ref.shape[0]):
        da_ref[:, p * BAND : (p + 1) * BAND] = dot_nn(d1, wo_ref[p]).astype(jnp.bfloat16)


def first_back(d_query, dz2, hat, scale, w_query, w_out, gain):
    height, width = d_query.shape
    tile = pl.BlockSpec((ROWS, width), lambda i: (i, 0))
    low = jax.ShapeDtypeStruct((height, width), jnp.bfloat16)
    return pl.pallas_call(
        first_back_kernel,
        out_shape=(
            jax.ShapeDtypeStruct((height, width), jnp.float32), low, low,
            jax.ShapeDtypeStruct((2, 8, width), jnp.float32),
        ),
        grid=(height // ROWS,),
        in_specs=[
            tile, tile, tile, pl.BlockSpec((ROWS, LANES), lambda i: (i, 0)), whole(w_query.shape),
            whole(w_out.shape), whole(gain.shape),
        ],
        out_specs=[tile, tile, tile, pl.BlockSpec((2, 8, width), lambda i: (0, 0, 0))],
        compiler_params=params(),
        cost_estimate=cost(4 * height * width * width, 16 * height * width),
        name="first_back",
    )(d_query, dz2, hat, scale, w_query, w_out, gain)


def pair_back_kernel(dk_ref, dv_ref, wk_ref, wv_ref, out_ref):
    out_ref[...] = (sum_bands_nt(dk_ref[...], wk_ref) + sum_bands_nt(dv_ref[...], wv_ref)).astype(out_ref.dtype)


def pair_back(d_key, d_value, w_key, w_value):
    height, width = d_key.shape
    tile = pl.BlockSpec((ROWS, width), lambda i: (i, 0))
    return pl.pallas_call(
        pair_back_kernel,
        out_shape=jax.ShapeDtypeStruct((height, width), jnp.bfloat16),
        grid=(height // ROWS,),
        in_specs=[tile, tile, whole(w_key.shape), whole(w_value.shape)],
        out_specs=tile,
        compiler_params=params(),
        cost_estimate=cost(4 * height * width * width, 6 * height * width),
        name="pair_back",
    )(d_key, d_value, w_key, w_value)


def tokens_kernel(main_tiles, dz1_ref, dq_ref, dk_ref, dv_ref, *refs):
    mains, (wq_ref, wk_ref, wv_ref, out_ref) = refs[:-4], refs[-4:]
    total = dz1_ref[...] + sum_bands_nt(dq_ref[...], wq_ref)

    @pl.when(pl.program_id(0) < main_tiles)
    def _():
        out_ref[...] = total + sum(main_ref[...].astype(jnp.float32) for main_ref in mains)

    @pl.when(pl.program_id(0) >= main_tiles)
    def _():
        out_ref[...] = total + sum_bands_nt(dk_ref[...], wk_ref) + sum_bands_nt(dv_ref[...], wv_ref)


def tokens_back(dz1, d_query, d_key, d_value, mains, weights):
    height, width = dz1.shape
    skip = mains[-1].shape[0] // ROWS
    tile = pl.BlockSpec((ROWS, width), lambda i: (i, 0))
    later = pl.BlockSpec((ROWS, width), lambda i: (jnp.maximum(i - skip, 0), 0))
    early = pl.BlockSpec((ROWS, width), lambda i: (jnp.minimum(i, skip - 1), 0))
    return pl.pallas_call(
        functools.partial(tokens_kernel, skip),
        out_shape=jax.ShapeDtypeStruct((height, width), jnp.float32),
        grid=(height // ROWS,),
        in_specs=[tile, tile, later, later] + [early] * len(mains) + [whole(weights[0].shape)] * 3,
        out_specs=tile,
        compiler_params=params(),
        cost_estimate=cost(6 * height * width * width, 16 * height * width),
        name="tokens_back",
    )(dz1, d_query, d_key, d_value, *mains, *weights)


def turn(target, source, at=0):
    height = source.shape[0]
    step = min(height, 512)
    for r in range(0, height, step):
        target[:, at + r : at + r + step] = source[r : r + step, :].astype(jnp.float32).T.astype(jnp.bfloat16)


def grad_feed_kernel(low_ref, d3_ref, du_ref, hid_ref, out_ref, low_t, d3_t):
    half = pl.num_programs(1) // 2

    @pl.when((pl.program_id(0) == 0) & (pl.program_id(1) == 0))
    def _():
        turn(low_t, low_ref)
        turn(d3_t, d3_ref)

    @pl.when(pl.program_id(1) < half)
    def _():
        out_ref[...] = dot_nn(low_t[...], du_ref[...]).astype(jnp.bfloat16)

    @pl.when(pl.program_id(1) >= half)
    def _():
        out_ref[...] = dot_nn(d3_t[...], hid_ref[...]).astype(jnp.bfloat16)


def grad_feed(low, d3, du, hid, parts):
    height, width = low.shape
    total = du.shape[1]
    half = total // parts // BAND
    return pl.pallas_call(
        grad_feed_kernel,
        out_shape=jax.ShapeDtypeStruct((width, 2 * total), jnp.bfloat16),
        grid=(parts, 2 * half),
        in_specs=[
            whole((height, width)), whole((height, width)),
            pl.BlockSpec((height, BAND), lambda p, c: (0, p * half + jnp.minimum(c, half - 1))),
            pl.BlockSpec((height, BAND), lambda p, c: (0, p * half + jnp.maximum(c - half, 0))),
        ],
        out_specs=pl.BlockSpec((width, BAND), lambda p, c: (0, p * 2 * half + c)),
        scratch_shapes=[pltpu.VMEM((width, height), jnp.bfloat16)] * 2,
        compiler_params=params(),
        cost_estimate=cost(4 * height * width * total, 4 * height * total + 4 * width * total),
        name="grad_feed",
    )(low, d3, du, hid)


def grad_pack_kernel(plan, counts, *refs):
    x_count = sum(counts)
    xs, rest = refs[:x_count], refs[x_count:]
    y_count = sum(len(terms) for terms in plan)
    ys, rest = rest[:y_count], rest[y_count:]
    out_ref, turned = rest[0], rest[1:]

    @pl.when(pl.program_id(0) == 0)
    def _():
        which = 0
        for target, count in zip(turned, counts):
            at = 0
            for source in xs[which : which + count]:
                turn(target, source, at)
                at += source.shape[0]
            which += count

    at = 0
    for n, terms in enumerate(plan):
        total = None
        for which, skip in terms:
            part = dot_nn(turned[which][:, skip:], ys[at][...])
            total = part if total is None else total + part
            at += 1
        out_ref[:, n * BAND : (n + 1) * BAND] = total.astype(jnp.bfloat16)


def grad_pack(groups, plan, ys):
    xs = [piece for group in groups for piece in group]
    width = xs[0].shape[1]
    parts = ys[0].shape[1] // BAND
    columns = len(plan) * BAND
    flops = sum(2 * y.shape[0] * width * y.shape[1] for y in ys)
    return pl.pallas_call(
        functools.partial(grad_pack_kernel, plan, tuple(len(group) for group in groups)),
        out_shape=jax.ShapeDtypeStruct((width, parts * columns), jnp.bfloat16),
        grid=(parts,),
        in_specs=[whole(x.shape) for x in xs] + [pl.BlockSpec((y.shape[0], BAND), lambda p: (0, p)) for y in ys],
        out_specs=pl.BlockSpec((width, columns), lambda p: (0, p)),
        scratch_shapes=[
            pltpu.VMEM((width, sum(piece.shape[0] for piece in group)), jnp.bfloat16) for group in groups
        ],
        compiler_params=params(),
        cost_estimate=cost(flops, sum(2 * y.size for y in ys) + 2 * width * parts * columns),
        name="grad_pack",
    )(*xs, *ys)


MESH_ID = pl.DeviceIdType.MESH


def gather_kernel(count, extra, fsdp_count, tp_count, *refs):
    locals_, extras, rest = refs[:count], refs[count : count + extra], refs[count + extra :]
    outs, rest = rest[:count], rest[count:]
    moved, rest = rest[: extra * (tp_count - 1)], rest[extra * (tp_count - 1) :]
    (
        own_sem, ring_send, ring_recv, fold_send, fold_recv, twin_send, twin_recv, move_send, move_recv
    ) = rest
    f_me, p_me = lax.axis_index("fsdp"), lax.axis_index("tp")
    bits = fsdp_count.bit_length() - 1
    outer = list(range(1, bits))
    orders = (outer, outer[::-1])
    rows = locals_[0].shape[0]
    half = rows // 2

    def toward(mask):
        return {"fsdp": lax.bitwise_xor(f_me, mask)}

    barrier = pltpu.get_barrier_semaphore()
    for k in range(1, tp_count):
        pl.semaphore_signal(
            barrier, inc=1, device_id={"tp": lax.rem(p_me + k, tp_count)}, device_id_type=MESH_ID
        )
    for b in range(bits):
        pl.semaphore_signal(barrier, inc=1, device_id=toward(1 << b), device_id_type=MESH_ID)
    pl.semaphore_wait(barrier, tp_count - 1 + bits)

    def span(f, h):
        return pl.ds(pl.multiple_of(f * rows + h * half, half), half)

    def ring(x, k):
        return pltpu.make_async_remote_copy(
            src_ref=locals_[x],
            dst_ref=outs[x].at[p_me, pl.ds(pl.multiple_of(f_me * rows, rows), rows)],
            send_sem=ring_send.at[x, k - 1],
            recv_sem=ring_recv.at[x, k - 1],
            device_id={"tp": lax.rem(p_me + k, tp_count)},
            device_id_type=MESH_ID,
        )

    def own(x):
        return pltpu.make_async_copy(
            locals_[x], outs[x].at[p_me, pl.ds(pl.multiple_of(f_me * rows, rows), rows)], own_sem.at[x]
        )

    def masks(order, stage):
        found = [0]
        for b in order[:stage]:
            found = found + [m | (1 << b) for m in found]
        return found

    def fold(x, h, stage, n):
        place = outs[x].at[:, span(lax.bitwise_xor(f_me, masks(orders[h], stage)[n]), h)]
        return pltpu.make_async_remote_copy(
            src_ref=place,
            dst_ref=place,
            send_sem=fold_send.at[x, h, (1 << stage) - 1 + n],
            recv_sem=fold_recv.at[x, h, (1 << stage) - 1 + n],
            device_id=toward(1 << orders[h][stage]),
            device_id_type=MESH_ID,
        )

    def twin(x, h, n):
        place = outs[x].at[:, span(lax.bitwise_xor(f_me, masks(orders[h], len(outer))[n]), h)]
        return pltpu.make_async_remote_copy(
            src_ref=place,
            dst_ref=place,
            send_sem=twin_send.at[x, h, n],
            recv_sem=twin_recv.at[x, h, n],
            device_id=toward(1),
            device_id_type=MESH_ID,
        )

    def move(e, k):
        return pltpu.make_async_remote_copy(
            src_ref=extras[e],
            dst_ref=moved[e * (tp_count - 1) + k - 1],
            send_sem=move_send.at[e, k - 1],
            recv_sem=move_recv.at[e, k - 1],
            device_id={"tp": lax.rem(p_me + k, tp_count)},
            device_id_type=MESH_ID,
        )

    stages = len(outer)
    for x in range(count):
        own(x).start()
        for k in range(1, tp_count):
            ring(x, k).start()
    for e in range(extra):
        for k in range(1, tp_count):
            move(e, k).start()
    for tick in range(count + stages + 1):
        for x in range(count):
            stage = tick - x
            if stage == 0:
                own(x).wait()
                for k in range(1, tp_count):
                    ring(x, k).wait_recv()
            if 0 < stage <= stages:
                for h in range(2):
                    for n in range(1 << (stage - 1)):
                        fold(x, h, stage - 1, n).wait_recv()
            if 0 <= stage < stages:
                for h in range(2):
                    for n in range(1 << stage):
                        fold(x, h, stage, n).start()
            if 0 <= stage <= stages:
                low = 0 if stage == 0 else 1 << (stage - 1)
                for h in range(2):
                    for n in range(low, 1 << stage):
                        twin(x, h, n).start()
    for x in range(count):
        for k in range(1, tp_count):
            ring(x, k).wait_send()
        for h in range(2):
            for stage in range(stages):
                for n in range(1 << stage):
                    fold(x, h, stage, n).wait_send()
            for n in range(1 << stages):
                twin(x, h, n).wait()
    for e in range(extra):
        for k in range(1, tp_count):
            move(e, k).wait()


def gather_weights(packs, extras, fsdp_count, tp_count, collective):
    rows = packs[0].shape[0]
    count = len(packs)
    outer = fsdp_count // 2
    extra = len(extras)
    results = pl.pallas_call(
        functools.partial(gather_kernel, count, extra, fsdp_count, tp_count),
        out_shape=tuple(
            jax.ShapeDtypeStruct((tp_count, fsdp_count * rows, pack.shape[1]), pack.dtype) for pack in packs
        )
        + tuple(jax.ShapeDtypeStruct(e.shape, e.dtype) for e in extras for _ in range(tp_count - 1)),
        in_specs=[pl.BlockSpec(memory_space=pltpu.VMEM)] * (count + extra),
        out_specs=[pl.BlockSpec(memory_space=pl.ANY)] * (count + extra * (tp_count - 1)),
        scratch_shapes=[
            pltpu.SemaphoreType.DMA((count,)),
            pltpu.SemaphoreType.DMA((count, tp_count - 1)),
            pltpu.SemaphoreType.DMA((count, tp_count - 1)),
            pltpu.SemaphoreType.DMA((count, 2, outer - 1)),
            pltpu.SemaphoreType.DMA((count, 2, outer - 1)),
            pltpu.SemaphoreType.DMA((count, 2, outer)),
            pltpu.SemaphoreType.DMA((count, 2, outer)),
            pltpu.SemaphoreType.DMA((extra, tp_count - 1)),
            pltpu.SemaphoreType.DMA((extra, tp_count - 1)),
        ],
        compiler_params=pltpu.CompilerParams(
            collective_id=collective, has_side_effects=True, vmem_limit_bytes=vmem_limit
        ),
        name="gather_weights",
    )(*packs, *extras)
    moved = results[count:]
    pieces = [
        [e] + list(moved[n * (tp_count - 1) : (n + 1) * (tp_count - 1)]) for n, e in enumerate(extras)
    ]
    return results[:count], pieces


def settle_kernel(count, fsdp_count, tp_count, main_ref, enc_ref, small_ref, *refs):
    packs, rest = refs[:count], refs[count:]
    mains, rest = rest[: tp_count - 1], rest[tp_count - 1 :]
    encs, rest = rest[: tp_count - 1], rest[tp_count - 1 :]
    total_ref, rest = rest[0], rest[1:]
    outs, rest = rest[:count], rest[count:]
    accs, rest = rest[:count], rest[count:]
    twins, rest = rest[:count], rest[count:]
    folds, rest = rest[:count], rest[count:]
    rings, rest = rest[:count], rest[count:]
    (
        small_box, twin_send, twin_recv, fold_send, fold_recv, ring_send, ring_recv,
        move_send, move_recv, small_send, small_recv,
    ) = rest
    f_me, p_me = lax.axis_index("fsdp"), lax.axis_index("tp")
    bits = fsdp_count.bit_length() - 1
    tp_bits = tp_count.bit_length() - 1
    outer = list(range(1, bits))
    slots = fsdp_count // 2
    orders = (outer, outer[::-1])
    rows = packs[0].shape[0] // fsdp_count

    def toward(mask):
        return {"fsdp": lax.bitwise_xor(f_me, mask)}

    def across(mask):
        return {"tp": lax.bitwise_xor(p_me, mask)}

    barrier = pltpu.get_barrier_semaphore()
    for k in range(1, tp_count):
        pl.semaphore_signal(
            barrier, inc=1, device_id={"tp": lax.rem(p_me + k, tp_count)}, device_id_type=MESH_ID
        )
    for b in range(bits):
        pl.semaphore_signal(barrier, inc=1, device_id=toward(1 << b), device_id_type=MESH_ID)
    pl.semaphore_wait(barrier, tp_count - 1 + bits)

    def copy(source, target, send, recv, device):
        return pltpu.make_async_remote_copy(
            src_ref=source, dst_ref=target, send_sem=send, recv_sem=recv, device_id=device,
            device_id_type=MESH_ID,
        )

    def block(ref, f):
        return ref.at[pl.ds(pl.multiple_of(f * rows, rows), rows)]

    def twin(x, n):
        other = lax.bitwise_xor(f_me, 1 ^ (2 * n))
        return copy(
            block(packs[x], other), twins[x].at[n], twin_send.at[x, n], twin_recv.at[x, n], toward(1)
        )

    def part(x, h):
        half = packs[x].shape[1] // 2
        return slice(h * half, (h + 1) * half)

    def kept(h, stage):
        found = [0]
        for b in orders[h][stage:]:
            found = found + [m | (1 << b) for m in found]
        return found

    def fold(x, h, stage, n):
        bit = 1 << orders[h][stage]
        keep = kept(h, stage + 1)[n]
        at = sum(slots >> (s + 1) for s in range(stage)) + n
        return copy(
            accs[x].at[(keep | bit) // 2, :, part(x, h)],
            folds[x].at[h, at],
            fold_send.at[x, h, at],
            fold_recv.at[x, h, at],
            toward(bit),
        )

    def ring(x, k):
        columns = packs[x].shape[1] // tp_count
        to = lax.rem(p_me + k, tp_count)
        return copy(
            accs[x].at[0, :, pl.ds(pl.multiple_of(to * columns, columns), columns)],
            rings[x].at[k - 1],
            ring_send.at[x, k - 1],
            ring_recv.at[x, k - 1],
            {"tp": to},
        )

    def move(e, k):
        source, targets = ((main_ref, mains), (enc_ref, encs))[e]
        to = lax.rem(p_me + tp_count - k, tp_count)
        return copy(
            source.at[k], targets[k - 1], move_send.at[e, k - 1], move_recv.at[e, k - 1], {"tp": to}
        )

    def small(stage):
        to = toward(1 << stage) if stage < bits else across(1 << (stage - bits))
        return copy(
            small_box.at[stage], small_box.at[bits + tp_bits + stage], small_send.at[stage],
            small_recv.at[stage], to,
        )

    stages = len(outer)
    for x in range(count):
        for n in range(slots):
            twin(x, n).start()
    for e in range(2):
        for k in range(1, tp_count):
            move(e, k).start()
    small_box[0] = small_ref[...]
    small(0).start()
    low = jnp.bfloat16
    for tick in range(count + stages + 1):
        for x in range(count):
            stage = tick - x
            if stage == 0:
                for n in range(slots):
                    twin(x, n).wait_recv()
                    mine = lax.bitwise_xor(f_me, 2 * n)
                    accs[x][n] = (
                        block(packs[x], mine)[...].astype(jnp.float32) + twins[x][n].astype(jnp.float32)
                    ).astype(low)
            if 0 < stage <= stages:
                for h in range(2):
                    for n in range(slots >> stage):
                        done = fold(x, h, stage - 1, n)
                        done.wait_send()
                        done.wait_recv()
                        at = sum(slots >> (s + 1) for s in range(stage - 1)) + n
                        where = kept(h, stage)[n] // 2
                        accs[x][where, :, part(x, h)] = (
                            accs[x][where, :, part(x, h)].astype(jnp.float32)
                            + folds[x][h, at].astype(jnp.float32)
                        ).astype(low)
            if 0 <= stage < stages:
                for h in range(2):
                    for n in range(slots >> (stage + 1)):
                        fold(x, h, stage, n).start()
            if stage == stages:
                for k in range(1, tp_count):
                    ring(x, k).start()
    for stage in range(bits + tp_bits):
        small(stage).wait()
        summed = small_box[stage] + small_box[bits + tp_bits + stage]
        if stage + 1 < bits + tp_bits:
            small_box[stage + 1] = summed
            small(stage + 1).start()
        else:
            total_ref[...] = summed
    for x in range(count):
        columns = packs[x].shape[1] // tp_count
        total = accs[x][0, :, pl.ds(pl.multiple_of(p_me * columns, columns), columns)].astype(jnp.float32)
        for k in range(1, tp_count):
            ring(x, k).wait()
            total = total + rings[x][k - 1].astype(jnp.float32)
        outs[x][...] = total
        for n in range(slots):
            twin(x, n).wait_send()
    for e in range(2):
        for k in range(1, tp_count):
            move(e, k).wait()


def settle(main_part, encoder_part, small, packs, fsdp_count, tp_count, collective):
    count = len(packs)
    bits = fsdp_count.bit_length() - 1 + tp_count.bit_length() - 1
    slots = fsdp_count // 2
    rows = packs[0].shape[0] // fsdp_count
    one = tp_count - 1
    low = jnp.bfloat16
    vmem = pl.BlockSpec(memory_space=pltpu.VMEM)
    away = pl.BlockSpec(memory_space=pl.ANY)
    results = pl.pallas_call(
        functools.partial(settle_kernel, count, fsdp_count, tp_count),
        out_shape=tuple(
            [jax.ShapeDtypeStruct(main_part.shape[1:], low)] * one
            + [jax.ShapeDtypeStruct(encoder_part.shape[1:], low)] * one
            + [jax.ShapeDtypeStruct(small.shape, small.dtype)]
            + [jax.ShapeDtypeStruct((rows, pack.shape[1] // tp_count), jnp.float32) for pack in packs]
        ),
        in_specs=[away, away, vmem] + [vmem] * count,
        out_specs=[away] * (2 * one) + [vmem] * (1 + count),
        scratch_shapes=[pltpu.VMEM((slots, rows, pack.shape[1]), low) for pack in packs]
        + [pltpu.VMEM((slots, rows, pack.shape[1]), low) for pack in packs]
        + [pltpu.VMEM((2, slots - 1, rows, pack.shape[1] // 2), low) for pack in packs]
        + [pltpu.VMEM((one, rows, pack.shape[1] // tp_count), low) for pack in packs]
        + [
            pltpu.VMEM((2 * bits,) + small.shape, jnp.float32),
            pltpu.SemaphoreType.DMA((count, slots)),
            pltpu.SemaphoreType.DMA((count, slots)),
            pltpu.SemaphoreType.DMA((count, 2, slots - 1)),
            pltpu.SemaphoreType.DMA((count, 2, slots - 1)),
            pltpu.SemaphoreType.DMA((count, one)),
            pltpu.SemaphoreType.DMA((count, one)),
            pltpu.SemaphoreType.DMA((2, one)),
            pltpu.SemaphoreType.DMA((2, one)),
            pltpu.SemaphoreType.DMA((bits,)),
            pltpu.SemaphoreType.DMA((bits,)),
        ],
        compiler_params=pltpu.CompilerParams(
            collective_id=collective, has_side_effects=True, vmem_limit_bytes=vmem_limit
        ),
        name="settle",
    )(main_part, encoder_part, small, *packs)
    return (
        [main_part[0]] + list(results[:one]),
        [encoder_part[0]] + list(results[one : 2 * one]),
        results[2 * one],
        results[2 * one + 1 :],
    )


def on_device(
    tokens,
    encoded,
    out_cotangent,
    segment_start,
    segment_parent,
    query_weight,
    key_weight,
    value_weight,
    out_weight,
    cross_query,
    cross_key,
    cross_value,
    cross_out,
    expand_weight,
    expand_bias,
    reduce_weight,
    reduce_bias,
    norm_gain,
    norm_bias,
    bucket_table,
):
    streams, batch, row_count, width = tokens.shape
    tp_index = lax.axis_index("tp")
    tp_count = lax.axis_size("tp")
    fsdp_count = lax.axis_size("fsdp")
    height = streams * batch * row_count
    main_height = batch * row_count

    def gather_pack(*pieces):
        packed = jnp.concatenate(pieces, axis=1)
        full = lax.all_gather(packed[None], ("tp", "fsdp"), axis=0, tiled=True)
        return full.reshape(tp_count, width, packed.shape[1])

    def settle_fsdp(packed):
        return lax.psum_scatter(packed, "fsdp", scatter_dimension=0, tiled=True)

    def settle_tp(part):
        columns = part.shape[1] // tp_count
        part = jnp.moveaxis(part.reshape(part.shape[0], tp_count, columns), 1, 0)
        return lax.psum_scatter(part, "tp", scatter_dimension=0, tiled=True)[0]

    def natural(pieces):
        stacked = jnp.stack(pieces)
        return jnp.concatenate(
            [
                lax.dynamic_slice_in_dim(stacked, lax.rem(tp_index - j + tp_count, tp_count), 1, 0)
                for j in range(tp_count)
            ]
        )

    levels, heads_local = bucket_table.shape
    shared = jnp.concatenate([bucket_table.T.reshape(-1), expand_bias]).reshape(-1, LANES)
    pack_feed = gather_pack(expand_weight, reduce_weight.T)
    gathered, (main_rows, encoder_rows, shared) = gather_weights(
        (
            query_weight, key_weight, value_weight, out_weight.T, cross_query, cross_key, cross_value,
            cross_out.T,
        ),
        (tokens[0].reshape(main_height, width), encoded.reshape(-1, width), shared),
        fsdp_count,
        tp_count,
        1,
    )
    w_q, w_k, w_v, w_ot, w_cq, w_ck, w_cv, w_cot = gathered
    shared = natural(shared).reshape(tp_count, -1)
    table = shared[:, : levels * heads_local].reshape(tp_count * heads_local, levels)
    expand_full = shared[:, levels * heads_local :].reshape(-1)

    heads = table.shape[0]
    groups = heads // GROUP
    lines = jnp.concatenate([table, jnp.full((heads, LANES - levels), masked_value, jnp.float32)], axis=1)
    lines = jnp.pad(lines.reshape(groups, GROUP, LANES), ((0, 0), (0, 8 - GROUP), (0, 0)))
    level_zero = table[:, 0].reshape(groups, GROUP)
    zero_row = jnp.pad(level_zero[:, None, :], ((0, 0), (0, 7), (0, LANES - GROUP)))
    zero_column = jnp.pad(level_zero[:, :, None], ((0, 0), (0, 8 - GROUP), (0, LANES - 1)))
    index = [
        tree_index(tree_facts(segment_start[b], segment_parent[b]), tp_index, row_count)
        for b in range(batch)
    ]
    by_row, by_key, near = (jnp.stack(parts) for parts in zip(*index))
    flags = jnp.any(
        (by_key < MASK_SLOT).reshape(batch, TREE // row_count, row_count * row_count), axis=2
    ).astype(jnp.int32)

    own_rows = tokens.reshape(height, width)
    cot_rows = out_cotangent.reshape(height, width)
    shape_own = tokens.shape
    shape_later = (streams - 1, batch, row_count, width)
    shape_main = (tp_count, batch, row_count, width)
    shape_enc = (tp_count,) + encoded.shape

    query, key_own, value_own = project([own_rows], (w_q, w_k, w_v), (0, main_height, main_height))
    key_main, value_main = project(main_rows, (w_k, w_v), (0, 0))
    query, key_own, value_own = (
        query.reshape(shape_own), key_own.reshape(shape_later), value_own.reshape(shape_later)
    )
    key_main, value_main = key_main.reshape(shape_main), value_main.reshape(shape_main)
    attended, lse = self_forward(
        flags, query, key_main, value_main, key_own, value_own, by_key, lines, zero_column
    )
    hat1, scale1, first_low, cross_q = first_norm(
        attended.reshape(height, width), own_rows, w_ot, w_cq, norm_gain, norm_bias
    )
    cross_k, cross_v = project(encoder_rows, (w_ck, w_cv), (0, 0))
    cross_q, cross_k, cross_v = (
        cross_q.reshape(shape_own), cross_k.reshape(shape_enc), cross_v.reshape(shape_enc)
    )
    crossed, cross_lse = cross_forward(cross_q, cross_k, cross_v)
    layer_out, second_low, hidden, du, d3, d2, dz2, dc, feed_sums, expand_sums = feed(
        crossed.reshape(height, width), hat1, cot_rows, w_cot, pack_feed, norm_gain, norm_bias,
        expand_full, reduce_bias,
    )
    feed_packed, dc = lax.optimization_barrier((grad_feed(second_low, d3, du, hidden, tp_count), dc))
    feed_part = settle_fsdp(feed_packed)
    d_cq, d_ck, d_cv = cross_backward(
        cross_q, cross_k, cross_v, dc.reshape(shape_own), crossed, cross_lse
    )
    d_cq, d_ck, d_cv = d_cq.reshape(height, width), d_ck.reshape(-1, width), d_cv.reshape(-1, width)
    encoder_part = pair_back(d_ck, d_cv, w_ck, w_cv)
    dz1, d1, da, first_sums = first_back(d_cq, dz2, hat1, scale1, w_cq, w_ot, norm_gain)
    cross_packed, da = lax.optimization_barrier((
        grad_pack(
            ([first_low], encoder_rows, [d1], [d2]),
            (((0, 0),), ((1, 0),), ((1, 0),), ((2, 0),), ((3, 0),)),
            (d_cq, d_ck, d_cv, attended.reshape(height, width), crossed.reshape(height, width)),
        ),
        da,
    ))
    d_q, d_k, d_v, d_k_own, d_v_own, hist, score_total, own_total = self_backward(
        flags, query, key_main, value_main, key_own, value_own, da.reshape(shape_own), attended, lse,
        by_row, near, lines, zero_row,
    )
    d_q = d_q.reshape(height, width)
    d_k, d_v = d_k.reshape(-1, width), d_v.reshape(-1, width)
    d_k_own, d_v_own = d_k_own.reshape(-1, width), d_v_own.reshape(-1, width)
    main_part = pair_back(d_k, d_v, w_k, w_v)
    feed_part, d_q = lax.optimization_barrier((settle_tp(feed_part), d_q))
    feed_grad = feed_part.astype(jnp.float32)
    self_packed = grad_pack(
        ([own_rows], main_rows),
        (((0, 0),), ((1, 0), (0, main_height)), ((1, 0), (0, main_height))),
        (d_q, d_k, d_k_own, d_v, d_v_own),
    )
    near_sum = jnp.sum(hist, axis=(0, 3)).reshape(heads, LANES)
    far_sum = jnp.sum(score_total, axis=(0, 3, 4)).reshape(heads) - jnp.sum(
        near_sum[:, : edge_list[-1]], axis=1
    )
    own_sum = jnp.sum(own_total, axis=(0, 2))[:, :GROUP].reshape(heads)
    starts = tuple(range(16)) + edge_list
    table_rows = [jnp.sum(near_sum[:, a:b], axis=1) for a, b in zip(starts[:-1], starts[1:])] + [far_sum]
    table_rows[0] = table_rows[0] + own_sum
    sums = jnp.sum(feed_sums, axis=1)
    first = jnp.sum(first_sums, axis=1)
    small = jnp.concatenate(
        [
            jnp.stack([first[0], sums[3], sums[0], first[1], sums[4], sums[1], sums[2]]).reshape(-1),
            jnp.sum(expand_sums, axis=0),
            jnp.stack(table_rows).reshape(-1),
        ]
    ).reshape(-1, LANES)
    main_grads, encoder_pieces, small, (self_grad, cross_grad) = settle(
        main_part.reshape(tp_count, main_height, width),
        encoder_part.reshape(tp_count, -1, width),
        small,
        (self_packed, cross_packed),
        fsdp_count,
        tp_count,
        2,
    )
    encoder_grad = sum(piece.astype(jnp.float32) for piece in encoder_pieces).reshape(encoded.shape)
    small = small.reshape(-1)
    tokens_grad = tokens_back(dz1, d_q, d_k_own, d_v_own, main_grads, (w_q, w_k, w_v))

    edge = 7 * width
    vectors = small[:edge].reshape(7, width)
    expand_total = small[edge : edge + expand_full.shape[0]]
    table_total = small[edge + expand_full.shape[0] :].reshape(levels, heads)
    expand_local = expand_bias.shape[0]

    def cut(packed, at, turned=False):
        piece = packed[:, at : at + BAND]
        return piece.T if turned else piece

    half = feed_grad.shape[1] // 2
    return (
        layer_out.reshape(shape_own),
        tokens_grad.reshape(shape_own),
        encoder_grad,
        cut(self_grad, 0),
        cut(self_grad, BAND),
        cut(self_grad, 2 * BAND),
        cut(cross_grad, 3 * BAND, True),
        cut(cross_grad, 0),
        cut(cross_grad, BAND),
        cut(cross_grad, 2 * BAND),
        cut(cross_grad, 4 * BAND, True),
        feed_grad[:, :half],
        lax.dynamic_slice_in_dim(expand_total, tp_index * expand_local, expand_local, 0),
        feed_grad[:, half:].T,
        vectors[6],
        vectors[0:3],
        vectors[3:6],
        lax.dynamic_slice_in_dim(table_total, tp_index * heads_local, heads_local, 1),
    )


def solution(mesh):
    placed = (
        P(None, "fsdp", "tp", None),
        P("fsdp", "tp", None),
        P(None, "fsdp", "tp", None),
        P("fsdp", None),
        P("fsdp", None),
        P("fsdp", "tp"),
        P("fsdp", "tp"),
        P("fsdp", "tp"),
        P("tp", "fsdp"),
        P("fsdp", "tp"),
        P("fsdp", "tp"),
        P("fsdp", "tp"),
        P("tp", "fsdp"),
        P("fsdp", "tp"),
        P("tp"),
        P("tp", "fsdp"),
        P(),
        P(),
        P(),
        P(None, "tp"),
    )
    return jax.shard_map(
        on_device,
        mesh=mesh,
        in_specs=placed,
        out_specs=(
            P(None, "fsdp", "tp", None),
            P(None, "fsdp", "tp", None),
            P("fsdp", "tp", None),
            P("fsdp", "tp"),
            P("fsdp", "tp"),
            P("fsdp", "tp"),
            P("tp", "fsdp"),
            P("fsdp", "tp"),
            P("fsdp", "tp"),
            P("fsdp", "tp"),
            P("tp", "fsdp"),
            P("fsdp", "tp"),
            P("tp"),
            P("tp", "fsdp"),
            P(),
            P(),
            P(),
            P(None, "tp"),
        ),
        check_vma=False,
    )
```
